256 devices in a mesh: chan: 32 (over x, y, core), wide: 8 (over z).
Axes of the slice: x: 4, y: 4, z: 8, core: 2. Of those that a mesh axis runs over, the one named last changes fastest.
Arguments:
- conc_now: float32 [8, 64, 64, 1024], P(None, 'chan', None, 'wide'), may hold values from 0.01 to 1
- conc_prev: float32 [8, 64, 64, 1024], P(None, 'chan', None, 'wide'), may hold values from 0.1 to 1
- phi_prev: float32 [64, 64, 1024], P('chan', None, 'wide'), may hold values from -3 to 3
- owner: int32 [64, 64, 1024], P('chan', None, 'wide'), may hold values from 0 to 2048, as said below
- partner: int32 [2048], replicated, may hold values from 0 to 2047, each once
- valence: int32 [8], replicated, may hold values from -2 to 2
- diffusivity: float32 [8], replicated, may hold values from 0.2 to 1
Outputs:
- conc_next: float32 [8, 64, 64, 1024], P(None, 'chan', None, 'wide')
- potential: float32 [64, 64, 1024], P('chan', None, 'wide')
The draws below stay inside these ranges and needn't reach their ends.
Inputs may be any that keep to these rules, and one draw needn't show every extreme that they name: `owner`: the value 2048 marks a cell of no junction. The cells of one junction lie within one block of 2 cells along the length and 128 along the width, aligned with the grid. Some junctions own no cell. `partner`: every junction appears once.
All inputs are finite; a program needn't handle non-finite values.
Results may differ from the reference program's by a relative error of at most 0.00029.
Values sent between devices are 32-bit elements; how exact they have to be, the bound alone decides.
A program may use at most 128 MiB of HBM per device.

```python
import math
import jax
import jax.numpy as jnp
from jax import lax

SPECIES = 8
CX = 2
CY = 128
NZ = 64
JUNC_DEV = 8
SWEEPS = 4
OUTER = 1
NX = 64
NY = 1024
JUNCTIONS = 2048


def draw_owner(key, part):
    base = jax.random.fold_in(key, 11)
    keys = jax.random.split(base, 7)
    tile_width = CY // JUNC_DEV
    tiles_y = NY // tile_width
    labels = jax.random.permutation(keys[0], JUNCTIONS).astype(jnp.int32)
    vacant_count = max(1, JUNCTIONS // 16)
    active = labels < JUNCTIONS - vacant_count
    width_x = jax.random.randint(keys[1], (JUNCTIONS,), max(1, CX // 2), CX + 1)
    start_x = jax.random.randint(keys[2], (JUNCTIONS,), 0, CX - width_x + 1)
    width_y = jax.random.randint(keys[3], (JUNCTIONS,), max(1, tile_width // 2), tile_width + 1)
    start_y = jax.random.randint(keys[4], (JUNCTIONS,), 0, tile_width - width_y + 1)
    width_z = jax.random.randint(keys[5], (JUNCTIONS,), max(1, NZ // 2), NZ)
    start_z = jax.random.randint(keys[6], (JUNCTIONS,), 0, NZ - width_z + 1)
    cell_x = jnp.arange(NX, dtype=jnp.int32)[:, None, None]
    cell_z = jnp.arange(NZ, dtype=jnp.int32)[None, :, None]
    cell_y = jnp.arange(NY, dtype=jnp.int32)[None, None, :]
    tile = cell_x // CX * tiles_y + cell_y // tile_width
    local_x = cell_x % CX
    local_y = cell_y % tile_width
    inside = active[tile]
    inside = inside & (local_x >= start_x[tile]) & (local_x < start_x[tile] + width_x[tile])
    inside = inside & (local_y >= start_y[tile]) & (local_y < start_y[tile] + width_y[tile])
    inside = inside & (cell_z >= start_z[tile]) & (cell_z < start_z[tile] + width_z[tile])
    return jnp.where(inside, labels[tile], JUNCTIONS).astype(jnp.int32)


def draw_conc_now(key, part):
    base = jax.random.fold_in(key, 23)
    first_key, second_key = jax.random.split(base, 2)
    tile_width = CY // JUNC_DEV
    tiles_x = NX // CX
    tiles_y = NY // tile_width
    level = jnp.exp(jax.random.uniform(first_key, (SPECIES, tiles_x, 1, tiles_y), jnp.float32, math.log(0.1), 0.0))
    rough = jnp.exp(jax.random.uniform(second_key, (SPECIES, NX, NZ, NY), jnp.float32, math.log(0.1), 0.0))
    level_full = jnp.repeat(jnp.repeat(level, CX, axis=1), tile_width, axis=3)
    return (level_full * rough).astype(jnp.float32)


def place_ends(result, stream_key, smallest, high):
    place = [jax.random.randint(jax.random.fold_in(stream_key, axis), (), 0, length) for axis, length in enumerate(result.shape)]
    widest = result.shape.index(max(result.shape))
    neighbour = place[:widest] + [(place[widest] + 1) % result.shape[widest]] + place[widest + 1:]
    return result.at[tuple(place)].set(smallest).at[tuple(neighbour)].set(high)


def levels(key, extent, cuts, smallest, largest):
    level = 1.0
    for position, parts in cuts:
        draws = jax.random.uniform(jax.random.fold_in(jax.random.fold_in(key, 6), position), (parts,), jnp.float32, smallest / len(cuts), largest / len(cuts))
        level = level * jnp.repeat(jnp.exp(draws), extent[position] // parts).reshape((-1,) + (1,) * (len(extent) - 1 - position))
    return level


def normal_values(stream_key, extent, deviation, bound, pieces=(), held_as=jnp.bfloat16):
    level = levels(stream_key, extent, pieces, -0.22, 0.18) if pieces else 1.0
    entries = jax.random.normal(stream_key, extent, jnp.float32) * deviation * level
    return jnp.minimum(jnp.maximum(entries, -bound), bound).astype(held_as)


def setup_inputs(seed: int = 0) -> dict:
    key_list = jax.random.split(jax.random.key(seed), 8)
    conc_now = draw_conc_now(jax.random.fold_in(key_list[7], 71), 0)
    conc_prev = jnp.clip(jnp.exp(math.log(1.0) - 2.3025851 * jax.random.uniform(key_list[1], (SPECIES, NX, NZ, NY), jnp.float32) ** levels(key_list[1], (SPECIES, NX, NZ, NY), ((1, 32), (3, 8)), -0.2, 0.2)), 0.1, 1.0)
    phi_prev = normal_values(key_list[2], (NX, NZ, NY), 0.5, 3.0, ((0, 32), (2, 8)), jnp.float32)
    owner = draw_owner(jax.random.fold_in(key_list[7], 71), 0)
    partner = jax.random.permutation(key_list[4], JUNCTIONS).astype(jnp.int32)
    valence = place_ends(jax.random.randint(key_list[5], (SPECIES,), -2, 3), jax.random.fold_in(key_list[5], 1), -2, 2).astype(jnp.int32)
    diffusivity = jnp.clip(jnp.exp(jax.random.uniform(key_list[6], (SPECIES,), jnp.float32, math.log(0.2), math.log(1.0))), 0.2, 1.0)
    return {"conc_now": conc_now, "conc_prev": conc_prev, "phi_prev": phi_prev, "owner": owner, "partner": partner, "valence": valence, "diffusivity": diffusivity}


time_step = 0.5
coupling = 2.0
charge_scale = 0.05
conduct_ref = 1.5
highest = lax.Precision.HIGHEST

def sine_table(length):
    index = jnp.arange(length).astype(jnp.float32) + 1.0
    return math.sqrt(2.0 / (length + 1.0)) * jnp.sin(math.pi * index[:, None] * index[None, :] / (length + 1.0))

def eigen_values(length):
    index = jnp.arange(length).astype(jnp.float32) + 1.0
    return 2.0 - 2.0 * jnp.cos(math.pi * index / (length + 1.0))

def conductivity(concs, valence, diffusivity):
    charge_sq = (valence * valence).astype(jnp.float32)
    weights = charge_sq * diffusivity / jnp.sum((charge_sq + 1.0) * diffusivity)
    return 1.0 + lax.optimization_barrier(jnp.sum(weights[:, None, None, None] * concs * concs, axis=0))

def face_pairs(padded):
    return [padded[..., :-2, 1:-1, 1:-1], padded[..., 2:, 1:-1, 1:-1], padded[..., 1:-1, :-2, 1:-1], padded[..., 1:-1, 2:, 1:-1], padded[..., 1:-1, 1:-1, :-2], padded[..., 1:-1, 1:-1, 2:]]

def apply_operator(potential_field, sigma):
    phi_padded = jnp.pad(potential_field, 1)
    sigma_padded = jnp.pad(sigma, 1)
    applied = jnp.zeros_like(potential_field)
    for phi_near, sigma_near in zip(face_pairs(phi_padded), face_pairs(sigma_padded)):
        applied = applied + 0.5 * (sigma + sigma_near) * (potential_field - phi_near)
    return applied

def precondition(residual_field):
    length_all, depth_all, width_all = residual_field.shape
    table_x = sine_table(length_all)
    table_z = sine_table(depth_all)
    table_y = sine_table(width_all)
    spectrum = jnp.einsum('ax,xzy->azy', table_x, residual_field, precision=highest)
    spectrum = jnp.einsum('bz,azy->aby', table_z, spectrum, precision=highest)
    spectrum = jnp.einsum('azy,yc->azc', spectrum, table_y, precision=highest)
    scale_all = conduct_ref * (eigen_values(length_all)[:, None, None] + eigen_values(depth_all)[None, :, None] + eigen_values(width_all)[None, None, :])
    spectrum = spectrum / scale_all
    spectrum = jnp.einsum('ax,xzy->azy', table_x, spectrum, precision=highest)
    spectrum = jnp.einsum('bz,azy->aby', table_z, spectrum, precision=highest)
    return jnp.einsum('azy,yc->azc', spectrum, table_y, precision=highest)

def junction_source(concs, owner, partner):
    owners = jnp.minimum(owner.reshape(-1), JUNCTIONS)
    cell_rows = concs.reshape(SPECIES, -1).T
    junction_sums = jax.ops.segment_sum(cell_rows, owners, num_segments=JUNCTIONS + 1)
    cell_counts = jax.ops.segment_sum(jnp.ones(owners.shape, jnp.float32), owners, num_segments=JUNCTIONS + 1)
    means = junction_sums / jnp.maximum(cell_counts, 1.0)[:, None]
    own_means = means[:JUNCTIONS]
    table = coupling * (own_means[partner] - own_means)
    table = jnp.concatenate([table, jnp.zeros((1, SPECIES), jnp.float32)], axis=0)
    return table[owners].T.reshape(concs.shape)

def species_sweep(concs, potential_field, conc_now, conc_prev, source, valence, diffusivity):
    phi_padded = jnp.pad(potential_field, 1, mode='edge')
    phi_near_all = face_pairs(phi_padded)
    drift_all = valence.astype(jnp.float32) * diffusivity

    def one_species(items):
        conc_one, now_one, prev_one, source_one, drift_one, spread_one = items
        conc_padded = jnp.pad(conc_one, 1, mode='edge')
        diagonal_part = jnp.zeros_like(conc_one) + 1.5 / time_step
        gathered_terms = (4.0 * now_one - prev_one) / (2.0 * time_step) + source_one
        for conc_near, phi_near in zip(face_pairs(conc_padded), phi_near_all):
            velocity = drift_one * (potential_field - phi_near)
            diagonal_part = diagonal_part + spread_one + jnp.maximum(velocity, 0.0)
            gathered_terms = gathered_terms + (spread_one + jnp.maximum(-velocity, 0.0)) * conc_near
        return gathered_terms / diagonal_part
    return lax.map(one_species, (concs, conc_now, conc_prev, source, drift_all, diffusivity))

def reference(conc_now, conc_prev, phi_prev, owner, partner, valence, diffusivity):
    concs = conc_now
    potential_field = phi_prev
    for iteration in range(OUTER):
        sigma = conductivity(concs, valence, diffusivity)
        charge = charge_scale * lax.optimization_barrier(jnp.sum(valence.astype(jnp.float32)[:, None, None, None] * concs, axis=0))
        for sweep_step in range(SWEEPS):
            potential_field = potential_field + precondition(charge - apply_operator(potential_field, sigma))
        source = junction_source(concs, owner, partner)
        concs = species_sweep(concs, potential_field, conc_now, conc_prev, source, valence, diffusivity)
    return (concs, potential_field)
```

```python
import functools

import jax
import jax.numpy as jnp
import numpy as np
from jax import lax
from jax.experimental import pallas as pl
from jax.experimental.pallas import tpu as pltpu
from jax.sharding import PartitionSpec as P

SWEEPS = 4
charge_scale = 0.05
coupling = 2.0
conduct_ref = 1.5
LANES = 128
LEVELS = 16
ROWS_AT_ONCE = 4
MESH = pl.DeviceIdType.MESH
f32 = jnp.float32
bf16 = jnp.bfloat16


def sine_table(length):
    index = np.arange(length) + 1.0
    return np.sqrt(2.0 / (length + 1.0)) * np.sin(np.pi * np.outer(index, index) / (length + 1.0))


def eigen_values(length):
    return 2.0 - 2.0 * np.cos(np.pi * (np.arange(length) + 1.0) / (length + 1.0))


def halves(table):
    table = np.asarray(table, np.float32)
    high = table.astype(bf16)
    low = (table - high.astype(np.float32)).astype(bf16)
    return high, low


def make_tables(nc, cx, nz, cy):
    nx, nb = nc * cx, nz // nc
    qx, qz, qy = sine_table(nx), sine_table(nz), sine_table(cy)
    depth_to = np.zeros((nc, cx, nb, cx, nz))
    for x in range(cx):
        depth_to[:, x, :, x, :] = qz.reshape(nc, nb, nz)
    length_to = np.einsum("aX,bc->abXc", qx, np.eye(nb)) / conduct_ref
    length_back = np.zeros((nc, cx + 2, nb, nx, nb))
    for p in range(nc):
        for xx in range(cx + 2):
            place = cx * p + xx - 1
            if 0 <= place < nx:
                for b in range(nb):
                    length_back[p, xx, b, :, b] = qx[place]
    depth_back = np.zeros((cx + 2, nz, nc, cx + 2, nb))
    for xx in range(cx + 2):
        depth_back[xx, :, :, xx, :] = qz.reshape(nz, nc, nb)
    modes = nx * nb
    lam = eigen_values(nx)[:, None] + eigen_values(nz)[None, :]
    lam = lam.reshape(nx, nc, nb).transpose(1, 0, 2).reshape(nc, 1, modes)
    theta = np.arccosh(1.0 + lam / 2.0)
    return dict(
        depth_to=halves(depth_to.reshape(nc * cx * nb, cx * nz)),
        length_to=halves(length_to.reshape(modes, modes)),
        length_back=halves(length_back.reshape(nc * (cx + 2) * nb, modes)),
        length_back_f=np.asarray(length_back.reshape(nc * (cx + 2) * nb, modes), np.float32),
        depth_back=halves(depth_back.reshape((cx + 2) * nz, nc * (cx + 2) * nb)),
        width=halves(qy),
        lam=np.asarray(lam, np.float32),
        theta=np.asarray(theta, np.float32),
        lam_y=np.asarray(eigen_values(cy)[None, :], np.float32),
    )


def dot(a, b):
    return jnp.dot(a, b, preferred_element_type=f32)


def split(value):
    high = value.astype(bf16)
    return high, (value - high.astype(f32)).astype(bf16)


def product(table, value):
    high, low = split(value)
    return dot(table[0], high) + dot(table[1], high) + dot(table[0], low)


def product_right(value, table):
    high, low = split(value)
    return dot(high, table[0]) + dot(high, table[1]) + dot(low, table[0])


def iota(shape, dim):
    return lax.broadcasted_iota(jnp.int32, shape, dim)


def kernel(
    cfg,
    val_ref, dif_ref, conc_ref, prev_ref, phi_ref, own_ref, par_ref,
    lam_ref, theta_ref, lam_y_ref,
    dt_h, dt_l, lt_h, lt_l, lb_h, lb_l, lb_f, db_h, db_l, wy_h, wy_l,
    out_conc, out_phi,
    phi_e, faces, charge, tab_p, tab_m, tab_d, edge_h, edge_l, coef,
    send1, recv1, send_g, recv_g, send2, recv2,
    sig, cols, cols_in, plane_in, conc_in,
    jacc, jmean, jrecv, jsum, jwide, jpiece, jall, jtab, src,
    send_sem, recv_sem,
):
    nc, nw, cx, nz, cy = cfg
    nb = nz // nc
    rows = cx * nz
    modes = nc * cx * nb
    species = conc_ref.shape[0] // rows
    me_c = lax.axis_index("chan")
    me_w = lax.axis_index("wide")
    left_c, right_c = lax.rem(me_c + nc - 1, nc), lax.rem(me_c + 1, nc)
    left_w, right_w = lax.rem(me_w + nw - 1, nw), lax.rem(me_w + 1, nw)

    barrier = pltpu.get_barrier_semaphore()

    def greet_c(i, _):
        pl.semaphore_signal(barrier, inc=1, device_id={"chan": lax.rem(me_c + i, nc)}, device_id_type=MESH)
        return 0

    def greet_w(i, _):
        pl.semaphore_signal(barrier, inc=1, device_id={"wide": lax.rem(me_w + i, nw)}, device_id_type=MESH)
        return 0

    lax.fori_loop(1, nc, greet_c, 0)
    lax.fori_loop(1, nw, greet_w, 0)

    lane = iota((rows, cy), 1)
    row = iota((rows, cy), 0)
    depth = lax.rem(row, nz)
    at_first, at_last = lane == 0, lane == cy - 1
    top, bottom = depth == 0, depth == nz - 1

    val = [val_ref[s].astype(f32) for s in range(species)]
    dif = [dif_ref[s] for s in range(species)]
    total = jnp.zeros((rows, cy), f32)
    part = jnp.zeros((rows, cy), f32)
    weight_all = jnp.float32(0.0)
    for s in range(species):
        c = conc_ref[pl.ds(s * rows, rows), :]
        square = val[s] * val[s]
        weight_all = weight_all + (square + 1.0) * dif[s]
        part = part + (square * dif[s]) * c * c
        total = total + val[s] * c
    sigma = 1.0 + part / jnp.full((1, 1), weight_all, f32)
    sig[...] = sigma
    charge[...] = charge_scale * total
    phi = phi_ref[...]

    packed = jnp.zeros((rows, cy), f32)
    for k in range(species + 2):
        field = phi if k == 0 else sigma if k == 1 else conc_ref[pl.ds((k - 2) * rows, rows), :]
        packed = jnp.where(lane == k, pltpu.roll(field, k, 1) if k else field, packed)
        packed = jnp.where(lane == LEVELS + k, pltpu.roll(field, LEVELS + 1 + k, 1), packed)
    cols[...] = packed.T[: 2 * LEVELS]

    pl.semaphore_wait(barrier, nc - 1 + nw - 1)

    SEM_A, SEM_G, SEM_B = 0, SWEEPS, 2 * SWEEPS
    SEM_H = 3 * SWEEPS
    SEM_J = SEM_H + 8

    def remote(src, dst, k, axis, place):
        return pltpu.make_async_remote_copy(
            src_ref=src, dst_ref=dst, send_sem=send_sem.at[k], recv_sem=recv_sem.at[k],
            device_id={axis: place}, device_id_type=MESH,
        )

    halo = [
        remote(cols.at[pl.ds(0, LEVELS)], cols_in.at[1], SEM_H, "wide", left_w),
        remote(cols.at[pl.ds(LEVELS, LEVELS)], cols_in.at[0], SEM_H + 1, "wide", right_w),
        remote(sig.at[pl.ds(0, nz)], plane_in.at[1, 0], SEM_H + 2, "chan", left_c),
        remote(sig.at[pl.ds(rows - nz, nz)], plane_in.at[0, 0], SEM_H + 3, "chan", right_c),
        remote(phi_ref.at[pl.ds(0, nz)], plane_in.at[1, 1], SEM_H + 4, "chan", left_c),
        remote(phi_ref.at[pl.ds(rows - nz, nz)], plane_in.at[0, 1], SEM_H + 5, "chan", right_c),
    ]
    conc_halo = []
    for s in range(species):
        conc_halo += [
            remote(conc_ref.at[pl.ds(s * rows, nz)], conc_in.at[1, s], SEM_H + 6, "chan", left_c),
            remote(conc_ref.at[pl.ds((s + 1) * rows - nz, nz)], conc_in.at[0, s], SEM_H + 7, "chan", right_c),
        ]
    for copy in halo:
        copy.start()

    def spread(src, dst, k, axis):
        n, me = (nc, me_c) if axis == "chan" else (nw, me_w)

        def body(i, _):
            p = lax.rem(me + i, n)
            remote(src(p), dst.at[me], k, axis, p).start()
            return 0

        lax.fori_loop(1, n, body, 0)
        pltpu.make_async_copy(src(me), dst.at[me], recv_sem.at[k]).start()

    def arrived(dst, k):
        pltpu.make_async_copy(dst, dst, recv_sem.at[k]).wait()

    def left(ref, k, n):
        part_of = ref.at[pl.ds(0, n)]
        pltpu.make_async_copy(part_of, part_of, send_sem.at[k]).wait()

    theta_row = theta_ref[me_c]
    theta = jnp.broadcast_to(theta_row, (cy, modes)).T
    lam = jnp.broadcast_to(lam_ref[me_c], (cy, modes)).T
    tab_d[...] = 1.0 / (lam + lam_y_ref[...])
    place = iota((modes, cy), 1).astype(f32)
    power = lambda n: jnp.exp(-theta * n)
    tab_p[...] = power(place)
    tab_m[...] = power(cy - 1.0 - place)
    scale = 1.0 / (1.0 - power(2.0 * cy + 2.0))
    mlane = iota((modes, cy), 1)
    edge_left = (power(place + 1.0) - power(2.0 * cy + 1.0 - place)) * scale
    edge_right = (power(cy - place) - power(cy + 2.0 + place)) * scale
    for k, edge in enumerate((edge_left, edge_right)):
        high, low = split(edge)
        here = pl.ds(k * modes, modes)
        edge_h[here, pl.ds(0, cy)] = high
        edge_l[here, pl.ds(0, cy)] = low
        edge_h[here, pl.ds(cy, cy)] = jnp.where(mlane == (cy - 1 if k == 0 else 0), 1.0, 0.0).astype(bf16)
        edge_l[here, pl.ds(cy, cy)] = jnp.zeros((modes, cy), bf16)
    width1 = cy * nw + 1
    rowp = lambda n: jnp.exp(-theta_row * n)
    front = 1.0 / ((1.0 - rowp(2.0)) * (1.0 - rowp(2.0 * width1)))
    for k in range(2):
        at = (cy * me_w if k == 0 else cy * (me_w + 1) + 1).astype(f32)
        below = (1.0 - rowp(2.0 * (width1 - at))) * front
        above = (1.0 - rowp(2.0 * at)) * front
        for w in range(nw):
            lower = (w < me_w) if k == 0 else (w <= me_w)
            n_plus = jnp.where(lower, at + (cy * w + 2.0), cy * w + 2.0 - at)
            n_minus = jnp.where(lower, at - (cy * w + cy - 1.0), 2.0 * width1 - at - (cy * w + cy - 1.0))
            factor = jnp.where(lower, below, above)
            sign = jnp.where(lower, -1.0, 1.0)
            coef[k, w, 0:1, :] = sign * factor * rowp(n_plus)
            coef[k, w, 1:2, :] = -sign * factor * rowp(n_minus)

    for copy in halo:
        copy.wait_recv()
    wall_xl, wall_xr = me_c == 0, me_c == nc - 1
    wall_yl, wall_yr = me_w == 0, me_w == nw - 1
    keep_xl, keep_xr = jnp.where(wall_xl, 0.0, 1.0), jnp.where(wall_xr, 0.0, 1.0)
    keep_yl, keep_yr = jnp.where(wall_yl, 0.0, 1.0), jnp.where(wall_yr, 0.0, 1.0)
    stacked = jnp.concatenate(
        [cols_in[0], cols_in[1], jnp.zeros((cy - 2 * LEVELS, rows), f32)], axis=0
    )
    col_in = stacked.T

    def neighbours(field, plane_l, plane_r, col_l, col_r, edge):
        low = field if edge is None else jnp.zeros_like(field)
        return [
            jnp.concatenate([plane_l, field[: rows - nz]], axis=0),
            jnp.concatenate([field[nz:], plane_r], axis=0),
            jnp.where(top, low, pltpu.roll(field, 1, 0)),
            jnp.where(bottom, low, pltpu.roll(field, rows - 1, 0)),
            jnp.where(at_first, col_l, pltpu.roll(field, 1, 1)),
            jnp.where(at_last, col_r, pltpu.roll(field, cy - 1, 1)),
        ]

    near = neighbours(
        sigma, plane_in[0, 0] * keep_xl, plane_in[1, 0] * keep_xr,
        col_in[:, 1:2] * keep_yl, col_in[:, LEVELS + 1 : LEVELS + 2] * keep_yr, 0,
    )
    for k in range(6):
        faces[k] = 0.5 * (sigma + near[k])
    phi_e[0:nz, 0:cy] = plane_in[0, 1] * keep_xl
    phi_e[nz : nz + rows, 0:cy] = phi
    phi_e[nz + rows : 2 * nz + rows, 0:cy] = plane_in[1, 1] * keep_xr
    phi_e[0:nz, cy : 2 * cy] = jnp.zeros((nz, cy), f32)
    phi_e[nz + rows : 2 * nz + rows, cy : 2 * cy] = jnp.zeros((nz, cy), f32)
    zero = jnp.zeros((rows, cy), f32)
    phi_e[nz : nz + rows, cy : 2 * cy] = jnp.where(
        at_last, col_in[:, 0:1] * keep_yl, jnp.where(at_first, col_in[:, LEVELS : LEVELS + 1] * keep_yr, zero)
    )

    def phi_near(beyond):
        field = phi_e[nz : nz + rows, 0:cy]
        ring = phi_e[nz : nz + rows, cy : 2 * cy]
        low = field if beyond is None else jnp.zeros_like(field)
        return field, [
            phi_e[0:rows, 0:cy],
            phi_e[2 * nz : 2 * nz + rows, 0:cy],
            jnp.where(top, low, pltpu.roll(field, 1, 0)),
            jnp.where(bottom, low, pltpu.roll(field, rows - 1, 0)),
            pltpu.roll(jnp.where(at_last, ring, field), 1, 1),
            pltpu.roll(jnp.where(at_first, ring, field), cy - 1, 1),
        ]

    def one_hot(label):
        return jnp.where(iota((LANES, LANES), 0) == (label & (LANES - 1)), 1.0, 0.0).astype(bf16)

    def sum_rows(first, last):
        def body(i, acc):
            picks, values = [], []
            for t in range(ROWS_AT_ONCE):
                r = i * ROWS_AT_ONCE + t
                label = own_ref[pl.ds(r, 1), :]
                level = lax.shift_right_logical(label, 7)
                value = conc_ref[pl.ds(r, species, stride=rows), :]
                high = value.astype(bf16).astype(f32)
                low = value - high
                picks.append(one_hot(label))
                here = [level == n for n in range(LEVELS)]
                blocks = [jnp.where(here[n], high, 0.0) for n in range(LEVELS)]
                blocks += [jnp.where(here[n], low, 0.0) for n in range(LEVELS)]
                blocks.append(jnp.where(iota((LEVELS, LANES), 0) == level, 1.0, 0.0))
                values.append(jnp.concatenate(blocks, axis=0).astype(bf16))
            jacc[...] += lax.dot_general(
                jnp.concatenate(values, axis=1), jnp.concatenate(picks, axis=1),
                (((1,), (1,)), ((), ())), preferred_element_type=f32,
            )
            return acc

        lax.fori_loop(first // ROWS_AT_ONCE, last // ROWS_AT_ONCE, body, 0)

    def look_up(table, labels):
        pick = jnp.concatenate([one_hot(label) for label in labels], axis=1)
        found = dot(table, pick)
        half = LEVELS * species
        results = []
        for t, label in enumerate(labels):
            level = lax.shift_right_logical(label, 7)
            column = found[:, t * LANES : (t + 1) * LANES]
            result = jnp.zeros((species, LANES), f32)
            for n in range(LEVELS):
                both = column[n * species : (n + 1) * species] + column[half + n * species : half + (n + 1) * species]
                result = result + jnp.where(level == n, both, 0.0)
            results.append(result)
        return results

    def means():
        half = LEVELS * species
        count = jnp.maximum(jacc[2 * half : 2 * half + LEVELS, :], 1.0)
        blocks = []
        for n in range(LEVELS):
            here = slice(n * species, (n + 1) * species)
            there = slice(half + n * species, half + (n + 1) * species)
            blocks.append((jacc[here, :] + jacc[there, :]) / count[n : n + 1])
        jmean[...] = jnp.concatenate(blocks, axis=0).reshape(jmean.shape)
        spread(lambda p: jmean.at[p], jrecv, SEM_J, "chan")

    def means_chan():
        arrived(jrecv, SEM_J)
        jsum[...] = jnp.sum(jrecv[...], axis=0)
        spread(lambda p: jsum, jwide, SEM_J + 1, "wide")

    def means_wide():
        arrived(jwide, SEM_J + 1)
        jpiece[...] = jnp.sum(jwide[...], axis=0)
        spread(lambda p: jpiece, jall, SEM_J + 2, "chan")

    def junction_table():
        arrived(jall, SEM_J + 2)
        table = jall[...].reshape(LEVELS * species, LANES)
        both = jnp.concatenate(split(table), axis=0)
        blocks = []
        for n in range(0, LEVELS, 2):
            found = look_up(both, [par_ref[n : n + 1, :], par_ref[n + 1 : n + 2, :]])
            for t in range(2):
                here = slice((n + t) * species, (n + t + 1) * species)
                blocks.append(coupling * (found[t] - table[here]))
        jtab[...] = jnp.concatenate(split(jnp.concatenate(blocks, axis=0)), axis=0)

    def source_rows(first, last):
        def body(i, acc):
            labels = [own_ref[pl.ds(i * ROWS_AT_ONCE + t, 1), :] for t in range(ROWS_AT_ONCE)]
            for t, found in enumerate(look_up(jtab[...], labels)):
                src[pl.ds(i * ROWS_AT_ONCE + t, species, stride=rows), :] = found
            return acc

        lax.fori_loop(first // ROWS_AT_ONCE, last // ROWS_AT_ONCE, body, 0)

    def conc_near(s):
        c = conc_ref[pl.ds(s * rows, rows), :]
        plane_l = jnp.where(wall_xl, c[:nz], conc_in[0, s])
        plane_r = jnp.where(wall_xr, c[rows - nz :], conc_in[1, s])
        line = cols_in[0, pl.ds(s + 2, 1), :], cols_in[1, pl.ds(s + 2, 1), :]
        sides = [jnp.broadcast_to(one, (cy, rows)).T for one in line]
        col_l = jnp.where(wall_yl, c, sides[0])
        col_r = jnp.where(wall_yr, c, sides[1])
        return c, neighbours(c, plane_l, plane_r, col_l, col_r, None)

    def start_species():
        arrived(conc_in.at[1], SEM_H + 6)
        arrived(conc_in.at[0], SEM_H + 7)
        for s in range(species):
            c, near_c = conc_near(s)
            flow = near_c[0]
            for k in range(1, 6):
                flow = flow + near_c[k]
            here = pl.ds(s * rows, rows)
            src[here, :] = src[here, :] + (4.0 * c - prev_ref[here, :]) + dif[s] * flow

    quarter = rows // 4
    jacc[...] = jnp.zeros_like(jacc)

    def fill(sweep, spot):
        if sweep == 0:
            if spot == 1:
                for copy in conc_halo:
                    copy.start()
            sum_rows((0, quarter, 2 * quarter)[spot], (quarter, 2 * quarter, 3 * quarter)[spot])
        elif sweep == 1:
            if spot == 0:
                sum_rows(3 * quarter, rows)
                means()
            elif spot == 1:
                means_chan()
            else:
                means_wide()
        elif sweep == 2:
            if spot == 0:
                junction_table()
            elif spot == 1:
                source_rows(0, quarter)
            else:
                source_rows(quarter, 2 * quarter)
        else:
            if spot == 0:
                source_rows(2 * quarter, 3 * quarter)
            elif spot == 1:
                source_rows(3 * quarter, rows)
            else:
                start_species()

    pick_row = iota((8, 2 * cy), 0)
    pick_lane = iota((8, 2 * cy), 1)
    pick = jnp.where(
        ((pick_row == 0) & (pick_lane < cy)) | ((pick_row == 1) & (pick_lane >= cy)), 1.0, 0.0
    ).astype(bf16)
    nt = (((1,), (1,)), ((), ()))

    for sweep in range(SWEEPS):
        field, near = phi_near(0)
        residual = charge[...]
        for k in range(6):
            residual = residual - faces[k] * (field - near[k])
        send1[sweep] = product((dt_h[...], dt_l[...]), residual).reshape(send1.shape[1:])
        spread(lambda p: send1.at[sweep, p], recv1.at[sweep], SEM_A + sweep, "chan")
        fill(sweep, 0)
        arrived(recv1.at[sweep], SEM_A + sweep)
        force = product((lt_h[...], lt_l[...]), recv1[sweep].reshape(modes, cy))
        high, low = split(jnp.concatenate([force * tab_p[...], force * tab_m[...]], axis=1))
        moments = lax.dot_general(pick, high, nt, preferred_element_type=f32)
        moments = moments + lax.dot_general(pick, low, nt, preferred_element_type=f32)
        send_g[sweep] = moments[0:2]
        spread(lambda p: send_g.at[sweep], recv_g.at[sweep], SEM_G + sweep, "wide")
        width = (wy_h[...], wy_l[...])
        inner = product_right(product_right(force, width) * tab_d[...], width)
        inner = product((lb_h[...], lb_l[...]), inner)
        fill(sweep, 1)
        arrived(recv_g.at[sweep], SEM_G + sweep)
        got = recv_g[sweep]
        ends = [jnp.sum(jnp.sum(got * coef[k], axis=0), axis=0, keepdims=True) for k in range(2)]
        back = lb_f[...]
        high, low = split(jnp.concatenate([back * ends[0], back * ends[1]], axis=1))
        outer = dot(high, edge_h[...]) + dot(low, edge_h[...]) + dot(high, edge_l[...])
        outer = jnp.concatenate([outer[:, :cy] + inner, outer[:, cy:]], axis=1)
        send2[sweep] = outer.reshape(send2.shape[1:])
        spread(lambda p: send2.at[sweep, p], recv2.at[sweep], SEM_B + sweep, "chan")
        fill(sweep, 2)
        arrived(recv2.at[sweep], SEM_B + sweep)
        phi_e[...] += product((db_h[...], db_l[...]), recv2[sweep].reshape(nc * (cx + 2) * nb, 2 * cy))

    field, near = phi_near(None)
    out_phi[...] = field
    drops = []
    for k in range(6):
        drop = field - near[k]
        if k == 0:
            drop = jnp.where((row < nz) & wall_xl, 0.0, drop)
        elif k == 1:
            drop = jnp.where((row >= rows - nz) & wall_xr, 0.0, drop)
        elif k == 4:
            drop = jnp.where(at_first & wall_yl, 0.0, drop)
        elif k == 5:
            drop = jnp.where(at_last & wall_yr, 0.0, drop)
        drops.append(drop)
    ups = [jnp.maximum(drop, 0.0) for drop in drops]
    downs = [jnp.maximum(-drop, 0.0) for drop in drops]
    up_all = ups[0] + ups[1] + ups[2] + ups[3] + ups[4] + ups[5]
    down_all = downs[0] + downs[1] + downs[2] + downs[3] + downs[4] + downs[5]
    for k in range(6):
        faces[k] = ups[k]
        faces[6 + k] = downs[k]
    for s in range(species):
        c, near_c = conc_near(s)
        drift = val[s] * dif[s]
        plus, minus = jnp.maximum(drift, 0.0), jnp.maximum(-drift, 0.0)
        top_part = src[pl.ds(s * rows, rows), :]
        for k in range(6):
            top_part = top_part + (plus * faces[6 + k] + minus * faces[k]) * near_c[k]
        out_conc[pl.ds(s * rows, rows), :] = top_part / ((3.0 + 6.0 * dif[s]) + plus * up_all + minus * down_all)

    for copy in halo:
        copy.wait_send()
    for k in (6, 7):
        pltpu.make_async_copy(conc_in.at[0], conc_in.at[0], send_sem.at[SEM_H + k]).wait()
    for sweep in range(SWEEPS):
        left(send1.at[sweep], SEM_A + sweep, nc - 1)
        left(recv_g.at[sweep], SEM_G + sweep, nw - 1)
        left(send2.at[sweep], SEM_B + sweep, nc - 1)
    left(jmean, SEM_J, nc - 1)
    left(jwide, SEM_J + 1, nw - 1)
    left(jall, SEM_J + 2, nc - 1)


def per_device(sizes, conc_now, conc_prev, phi_prev, owner, partner, valence, diffusivity):
    nc, nw = sizes
    species, cx, nz, cy = conc_now.shape
    nb = nz // nc
    rows, modes = cx * nz, nc * cx * nb
    t = make_tables(nc, cx, nz, cy)
    tables = [t["lam"], t["theta"], t["lam_y"], *t["depth_to"], *t["length_to"], *t["length_back"],
              t["length_back_f"], *t["depth_back"], *t["width"]]
    ext = (cx + 2) * nz
    jrow = LEVELS * species // nc
    vmem = pl.BlockSpec(memory_space=pltpu.VMEM)
    smem = pl.BlockSpec(memory_space=pltpu.SMEM)
    sems = 3 * SWEEPS + 8 + 3
    out_conc, out_phi = pl.pallas_call(
        functools.partial(kernel, (nc, nw, cx, nz, cy)),
        out_shape=(
            jax.ShapeDtypeStruct((species * rows, cy), f32),
            jax.ShapeDtypeStruct((rows, cy), f32),
        ),
        in_specs=[smem, smem] + [vmem] * (5 + len(tables)),
        out_specs=(vmem, vmem),
        scratch_shapes=[
            pltpu.VMEM((ext, 2 * cy), f32),
            pltpu.VMEM((12, rows, cy), f32),
            pltpu.VMEM((rows, cy), f32),
            pltpu.VMEM((modes, cy), f32),
            pltpu.VMEM((modes, cy), f32),
            pltpu.VMEM((modes, cy), f32),
            pltpu.VMEM((2 * modes, 2 * cy), bf16),
            pltpu.VMEM((2 * modes, 2 * cy), bf16),
            pltpu.VMEM((2, nw, 2, modes), f32),
            pltpu.VMEM((SWEEPS, nc, cx * nb, cy), f32),
            pltpu.VMEM((SWEEPS, nc, cx * nb, cy), f32),
            pltpu.VMEM((SWEEPS, 2, modes), f32),
            pltpu.VMEM((SWEEPS, nw, 2, modes), f32),
            pltpu.VMEM((SWEEPS, nc, (cx + 2) * nb, 2 * cy), f32),
            pltpu.VMEM((SWEEPS, nc, (cx + 2) * nb, 2 * cy), f32),
            pltpu.VMEM((rows, cy), f32),
            pltpu.VMEM((2 * LEVELS, rows), f32),
            pltpu.VMEM((2, LEVELS, rows), f32),
            pltpu.VMEM((2, 2, nz, cy), f32),
            pltpu.VMEM((2, species, nz, cy), f32),
            pltpu.VMEM((LEVELS * (2 * species + 1), LANES), f32),
            pltpu.VMEM((nc, jrow, LANES), f32),
            pltpu.VMEM((nc, jrow, LANES), f32),
            pltpu.VMEM((jrow, LANES), f32),
            pltpu.VMEM((nw, jrow, LANES), f32),
            pltpu.VMEM((jrow, LANES), f32),
            pltpu.VMEM((nc, jrow, LANES), f32),
            pltpu.VMEM((2 * LEVELS * species, LANES), bf16),
            pltpu.VMEM((species * rows, cy), f32),
            pltpu.SemaphoreType.DMA((sems,)),
            pltpu.SemaphoreType.DMA((sems,)),
        ],
        compiler_params=pltpu.CompilerParams(
            collective_id=0, has_side_effects=True, vmem_limit_bytes=48 * 1024 * 1024
        ),
        name="step",
    )(
        valence,
        diffusivity,
        conc_now.reshape(species * rows, cy),
        conc_prev.reshape(species * rows, cy),
        phi_prev.reshape(rows, cy),
        owner.reshape(rows, cy),
        partner.reshape(LEVELS, LANES),
        *[jnp.asarray(one) for one in tables],
    )
    return out_conc.reshape(conc_now.shape), out_phi.reshape(phi_prev.shape)


def solution(mesh):
    return jax.shard_map(
        functools.partial(per_device, (mesh.shape["chan"], mesh.shape["wide"])),
        mesh=mesh,
        in_specs=(
            P(None, "chan", None, "wide"),
            P(None, "chan", None, "wide"),
            P("chan", None, "wide"),
            P("chan", None, "wide"),
            P(),
            P(),
            P(),
        ),
        out_specs=(P(None, "chan", None, "wide"), P("chan", None, "wide")),
        check_vma=False,
    )
```

```python
import functools

import jax
import jax.numpy as jnp
import numpy as np
from jax import lax
from jax.experimental import pallas as pl
from jax.experimental.pallas import tpu as pltpu
from jax.sharding import PartitionSpec as P

SWEEPS = 4
charge_scale = 0.05
coupling = 2.0
conduct_ref = 1.5
LANES = 128
LEVELS = 16
ROWS_AT_ONCE = 4
MESH = pl.DeviceIdType.MESH
f32 = jnp.float32
bf16 = jnp.bfloat16


def sine_table(length):
    index = np.arange(length) + 1.0
    return np.sqrt(2.0 / (length + 1.0)) * np.sin(np.pi * np.outer(index, index) / (length + 1.0))


def eigen_values(length):
    return 2.0 - 2.0 * np.cos(np.pi * (np.arange(length) + 1.0) / (length + 1.0))


def halves(table):
    table = np.asarray(table, np.float32)
    high = table.astype(bf16)
    low = (table - high.astype(np.float32)).astype(bf16)
    return high, low


def make_tables(nc, cx, nz, cy):
    nx, nb = nc * cx, nz // nc
    qx, qz, qy = sine_table(nx), sine_table(nz), sine_table(cy)
    depth_to = np.zeros((nc, cx, nb, cx, nz))
    for x in range(cx):
        depth_to[:, x, :, x, :] = qz.reshape(nc, nb, nz)
    length_to = np.einsum("aX,bc->abXc", qx, np.eye(nb)) / conduct_ref
    length_back = np.zeros((nc, cx + 2, nb, nx, nb))
    for p in range(nc):
        for xx in range(cx + 2):
            place = cx * p + xx - 1
            if 0 <= place < nx:
                for b in range(nb):
                    length_back[p, xx, b, :, b] = qx[place]
    depth_back = np.zeros((cx + 2, nz, nc, cx + 2, nb))
    for xx in range(cx + 2):
        depth_back[xx, :, :, xx, :] = qz.reshape(nz, nc, nb)
    depth_ring = np.zeros((cx, nz, cx, nb, nc))
    for x in range(cx):
        depth_ring[x, :, x, :, :] = qz.reshape(nz, nc, nb).transpose(0, 2, 1)
    length_ring = np.zeros((nc, cx, nx, nb))
    length_ring[:] = qx.reshape(nc, cx, nx)[..., None]
    modes = nx * nb
    lam = eigen_values(nx)[:, None] + eigen_values(nz)[None, :]
    lam = lam.reshape(nx, nc, nb).transpose(1, 0, 2).reshape(nc, 1, modes)
    theta = np.arccosh(1.0 + lam / 2.0)
    big = dict(
        dt=depth_to.reshape(nc * cx * nb, cx * nz),
        lt=length_to.reshape(modes, modes),
        lb=length_back.reshape(nc * (cx + 2) * nb, modes),
        db=depth_back.reshape((cx + 2) * nz, nc * (cx + 2) * nb),
        wy=qy,
        dr=depth_ring.reshape(cx * nz, cx * nb * nc),
        lr=length_ring.reshape(nc, cx * modes),
    )
    places, parts, row = {}, [], 0
    for name, table in big.items():
        for k, half in enumerate(halves(table)):
            height = -(-half.shape[0] // 32) * 32
            block = np.zeros((height, 2 * LANES), bf16)
            block[: half.shape[0], : half.shape[1]] = half
            parts.append(block)
            places[name, k] = (row, *half.shape)
            row += height
    small = np.zeros((nc, 8, max(modes, LANES)), np.float32)
    small[:, 0, :modes] = theta[:, 0]
    small[:, 1, :modes] = lam[:, 0]
    small[:, 2, :cy] = eigen_values(cy)
    return places, np.concatenate(parts, axis=0), small


def dot(a, b):
    return jnp.dot(a, b, preferred_element_type=f32)


def split(value):
    high = value.astype(bf16)
    return high, (value - high.astype(f32)).astype(bf16)


def product(table, value):
    high, low = split(value)
    return dot(table[0], high) + dot(table[1], high) + dot(table[0], low)


def product_right(value, table):
    high, low = split(value)
    return dot(high, table[0]) + dot(high, table[1]) + dot(low, table[0])


def iota(shape, dim):
    return lax.broadcasted_iota(jnp.int32, shape, dim)


def kernel(
    cfg, places,
    val_hbm, dif_hbm, conc_hbm, prev_hbm, phi_hbm, own_hbm, par_hbm, big_hbm, small_hbm,
    out_conc, out_phi,
    val_ref, dif_ref, conc_ref, prev_ref, phi_ref, own_ref, par_ref, big, small,
    phi_e, faces, charge, tab_p, tab_m, tab_d, edge_h, edge_l, coef,
    send1, recv1, send_g, recv_g, send2, recv2,
    sig, cols, cols_in, plane_in, conc_in,
    jacc, jmean, jrecv, jsum, jwide, jpiece, jall, jtab, src,
    send_sem, recv_sem, load_sem,
):
    nc, nw, cx, nz, cy = cfg
    nb = nz // nc
    rows = cx * nz
    modes = nc * cx * nb
    species = conc_ref.shape[0] // rows
    me_c = lax.axis_index("chan")
    me_w = lax.axis_index("wide")
    left_c, right_c = lax.rem(me_c + nc - 1, nc), lax.rem(me_c + 1, nc)
    left_w, right_w = lax.rem(me_w + nw - 1, nw), lax.rem(me_w + 1, nw)

    barrier = pltpu.get_barrier_semaphore()

    def greet_c(i, _):
        pl.semaphore_signal(barrier, inc=1, device_id={"chan": lax.rem(me_c + i, nc)}, device_id_type=MESH)
        return 0

    def greet_w(i, _):
        pl.semaphore_signal(barrier, inc=1, device_id={"wide": lax.rem(me_w + i, nw)}, device_id_type=MESH)
        return 0

    loads = {}
    for k, (name, there, here) in enumerate([
        ("small", small_hbm.at[me_c], small), ("val", val_hbm, val_ref), ("dif", dif_hbm, dif_ref),
        ("conc", conc_hbm, conc_ref), ("phi", phi_hbm, phi_ref), ("big", big_hbm, big),
        ("own", own_hbm, own_ref), ("par", par_hbm, par_ref), ("prev", prev_hbm, prev_ref),
    ]):
        loads[name] = pltpu.make_async_copy(there, here, load_sem.at[k])
        loads[name].start()
    lax.fori_loop(1, nc, greet_c, 0)
    lax.fori_loop(1, nw, greet_w, 0)

    def table(name):
        def half(k):
            row, height, width = places[name, k]
            return big[pl.ds(row, height), pl.ds(0, width)]
        return half(0), half(1)

    lane = iota((rows, cy), 1)
    row = iota((rows, cy), 0)
    depth = lax.rem(row, nz)
    at_first, at_last = lane == 0, lane == cy - 1
    top, bottom = depth == 0, depth == nz - 1

    loads["small"].wait()
    theta_row = small[0:1, 0:modes]
    theta = jnp.broadcast_to(theta_row, (cy, modes)).T
    lam = jnp.broadcast_to(small[1:2, 0:modes], (cy, modes)).T
    tab_d[...] = 1.0 / (lam + small[2:3, 0:cy])
    place = iota((modes, cy), 1).astype(f32)
    power = lambda n: jnp.exp(-theta * n)
    tab_p[...] = power(place)
    tab_m[...] = power(cy - 1.0 - place)
    scale = 1.0 / (1.0 - power(2.0 * cy + 2.0))
    edge_left = (power(place + 1.0) - power(2.0 * cy + 1.0 - place)) * scale
    edge_right = (power(cy - place) - power(cy + 2.0 + place)) * scale
    for k, edge in enumerate((edge_left, edge_right)):
        high, low = split(edge)
        here = pl.ds(k * modes, modes)
        edge_h[here, pl.ds(0, cy)] = high
        edge_l[here, pl.ds(0, cy)] = low
    width1 = cy * nw + 1
    rowp = lambda n: jnp.exp(-theta_row * n)
    front = 1.0 / ((1.0 - rowp(2.0)) * (1.0 - rowp(2.0 * width1)))
    for k in range(2):
        at = (cy * me_w if k == 0 else cy * (me_w + 1) + 1).astype(f32)
        below = (1.0 - rowp(2.0 * (width1 - at))) * front
        above = (1.0 - rowp(2.0 * at)) * front
        for w in range(nw):
            lower = (w < me_w) if k == 0 else (w <= me_w)
            n_plus = jnp.where(lower, at + (cy * w + 2.0), cy * w + 2.0 - at)
            n_minus = jnp.where(lower, at - (cy * w + cy - 1.0), 2.0 * width1 - at - (cy * w + cy - 1.0))
            factor = jnp.where(lower, below, above)
            sign = jnp.where(lower, -1.0, 1.0)
            coef[k, w, 0:1, :] = sign * factor * rowp(n_plus)
            coef[k, w, 1:2, :] = -sign * factor * rowp(n_minus)

    for name in ("val", "dif", "conc"):
        loads[name].wait()
    val = [val_ref[s].astype(f32) for s in range(species)]
    dif = [dif_ref[s] for s in range(species)]
    total = jnp.zeros((rows, cy), f32)
    part = jnp.zeros((rows, cy), f32)
    weight_all = jnp.float32(0.0)
    for s in range(species):
        c = conc_ref[pl.ds(s * rows, rows), :]
        square = val[s] * val[s]
        weight_all = weight_all + (square + 1.0) * dif[s]
        part = part + (square * dif[s]) * c * c
        total = total + val[s] * c
    sigma = 1.0 + part / jnp.full((1, 1), weight_all, f32)
    sig[...] = sigma
    charge[...] = charge_scale * total
    loads["phi"].wait()
    phi = phi_ref[...]

    packed = jnp.zeros((rows, cy), f32)
    for k in range(species + 2):
        field = phi if k == 0 else sigma if k == 1 else conc_ref[pl.ds((k - 2) * rows, rows), :]
        packed = jnp.where(lane == k, pltpu.roll(field, k, 1) if k else field, packed)
        packed = jnp.where(lane == LEVELS + k, pltpu.roll(field, LEVELS + 1 + k, 1), packed)
    cols[...] = packed.T[: 2 * LEVELS]

    pl.semaphore_wait(barrier, nc - 1 + nw - 1)

    SEM_A, SEM_G, SEM_B = 0, SWEEPS, 2 * SWEEPS
    SEM_H = 3 * SWEEPS
    SEM_J = SEM_H + 8

    def remote(src, dst, k, axis, place):
        return pltpu.make_async_remote_copy(
            src_ref=src, dst_ref=dst, send_sem=send_sem.at[k], recv_sem=recv_sem.at[k],
            device_id={axis: place}, device_id_type=MESH,
        )

    halo = [
        remote(cols.at[pl.ds(0, LEVELS)], cols_in.at[1], SEM_H, "wide", left_w),
        remote(cols.at[pl.ds(LEVELS, LEVELS)], cols_in.at[0], SEM_H + 1, "wide", right_w),
        remote(sig.at[pl.ds(0, nz)], plane_in.at[1, 0], SEM_H + 2, "chan", left_c),
        remote(sig.at[pl.ds(rows - nz, nz)], plane_in.at[0, 0], SEM_H + 3, "chan", right_c),
        remote(phi_ref.at[pl.ds(0, nz)], plane_in.at[1, 1], SEM_H + 4, "chan", left_c),
        remote(phi_ref.at[pl.ds(rows - nz, nz)], plane_in.at[0, 1], SEM_H + 5, "chan", right_c),
    ]
    conc_halo = []
    for s in range(species):
        conc_halo += [
            remote(conc_ref.at[pl.ds(s * rows, nz)], conc_in.at[1, s], SEM_H + 6, "chan", left_c),
            remote(conc_ref.at[pl.ds((s + 1) * rows - nz, nz)], conc_in.at[0, s], SEM_H + 7, "chan", right_c),
        ]
    for copy in halo:
        copy.start()

    if nc == 32:
        order = [(dx, dy, dc) for dx in range(4) for dy in range(4) for dc in range(2)]
        hops = (0, 1, 2, 1)
        order = sorted(order[1:], key=lambda o: -(hops[o[0]] + hops[o[1]]))
        at_x = [lax.rem(me_c // 8 + d, 4) * 8 for d in range(4)]
        at_y = [lax.rem(me_c // 2 + d, 4) * 2 for d in range(4)]
        at_core = [lax.rem(me_c + d, 2) for d in range(2)]
        peers_c = [at_x[dx] + at_y[dy] + at_core[dc] for dx, dy, dc in order]
    else:
        peers_c = [lax.rem(me_c + d, nc) for d in range(1, nc)]
    peers_w = [lax.rem(me_w + d, nw) for d in sorted(range(1, nw), key=lambda d: -min(d, nw - d))]

    def spread(src, dst, k, axis):
        n, me = (nc, me_c) if axis == "chan" else (nw, me_w)

        def body(i, _):
            p = lax.rem(me + i, n)
            remote(src(p), dst.at[me], k, axis, p).start()
            return 0

        lax.fori_loop(1, n, body, 0)
        pltpu.make_async_copy(src(me), dst.at[me], recv_sem.at[k]).start()

    def spread_fast(src, dst, k, axis):
        peers, me = (peers_c, me_c) if axis == "chan" else (peers_w, me_w)
        for p in peers:
            remote(src(p), dst.at[me], k, axis, p).start()
        pltpu.make_async_copy(src(me), dst.at[me], recv_sem.at[k]).start()

    def arrived(dst, k):
        pltpu.make_async_copy(dst, dst, recv_sem.at[k]).wait()

    def left(ref, k, n):
        part_of = ref.at[pl.ds(0, n)]
        pltpu.make_async_copy(part_of, part_of, send_sem.at[k]).wait()

    for copy in halo:
        copy.wait_recv()
    wall_xl, wall_xr = me_c == 0, me_c == nc - 1
    wall_yl, wall_yr = me_w == 0, me_w == nw - 1
    keep_xl, keep_xr = jnp.where(wall_xl, 0.0, 1.0), jnp.where(wall_xr, 0.0, 1.0)
    keep_yl, keep_yr = jnp.where(wall_yl, 0.0, 1.0), jnp.where(wall_yr, 0.0, 1.0)
    stacked = jnp.concatenate(
        [cols_in[0], cols_in[1], jnp.zeros((cy - 2 * LEVELS, rows), f32)], axis=0
    )
    col_in = stacked.T

    def neighbours(field, plane_l, plane_r, col_l, col_r, edge):
        low = field if edge is None else jnp.zeros_like(field)
        return [
            jnp.concatenate([plane_l, field[: rows - nz]], axis=0),
            jnp.concatenate([field[nz:], plane_r], axis=0),
            jnp.where(top, low, pltpu.roll(field, 1, 0)),
            jnp.where(bottom, low, pltpu.roll(field, rows - 1, 0)),
            jnp.where(at_first, col_l, pltpu.roll(field, 1, 1)),
            jnp.where(at_last, col_r, pltpu.roll(field, cy - 1, 1)),
        ]

    near = neighbours(
        sigma, plane_in[0, 0] * keep_xl, plane_in[1, 0] * keep_xr,
        col_in[:, 1:2] * keep_yl, col_in[:, LEVELS + 1 : LEVELS + 2] * keep_yr, 0,
    )
    for k in range(6):
        faces[k] = 0.5 * (sigma + near[k])
    phi_e[0:nz, 0:cy] = plane_in[0, 1] * keep_xl
    phi_e[nz : nz + rows, 0:cy] = phi
    phi_e[nz + rows : 2 * nz + rows, 0:cy] = plane_in[1, 1] * keep_xr
    phi_e[0:nz, cy : 2 * cy] = jnp.zeros((nz, cy), f32)
    phi_e[nz + rows : 2 * nz + rows, cy : 2 * cy] = jnp.zeros((nz, cy), f32)
    zero = jnp.zeros((rows, cy), f32)
    phi_e[nz : nz + rows, cy : 2 * cy] = jnp.where(
        at_last, col_in[:, 0:1] * keep_yl, jnp.where(at_first, col_in[:, LEVELS : LEVELS + 1] * keep_yr, zero)
    )

    def phi_near(beyond):
        field = phi_e[nz : nz + rows, 0:cy]
        ring = phi_e[nz : nz + rows, cy : 2 * cy]
        low = field if beyond is None else jnp.zeros_like(field)
        return field, [
            phi_e[0:rows, 0:cy],
            phi_e[2 * nz : 2 * nz + rows, 0:cy],
            jnp.where(top, low, pltpu.roll(field, 1, 0)),
            jnp.where(bottom, low, pltpu.roll(field, rows - 1, 0)),
            pltpu.roll(jnp.where(at_last, ring, field), 1, 1),
            pltpu.roll(jnp.where(at_first, ring, field), cy - 1, 1),
        ]

    def one_hot(label):
        return jnp.where(iota((LANES, LANES), 0) == (label & (LANES - 1)), 1.0, 0.0).astype(bf16)

    def sum_rows(first, last):
        def body(i, acc):
            picks, values = [], []
            for t in range(ROWS_AT_ONCE):
                r = i * ROWS_AT_ONCE + t
                label = own_ref[pl.ds(r, 1), :]
                level = lax.shift_right_logical(label, 7)
                value = conc_ref[pl.ds(r, species, stride=rows), :]
                high = value.astype(bf16).astype(f32)
                low = value - high
                picks.append(one_hot(label))
                here = [level == n for n in range(LEVELS)]
                blocks = [jnp.where(here[n], high, 0.0) for n in range(LEVELS)]
                blocks += [jnp.where(here[n], low, 0.0) for n in range(LEVELS)]
                blocks.append(jnp.where(iota((LEVELS, LANES), 0) == level, 1.0, 0.0))
                values.append(jnp.concatenate(blocks, axis=0).astype(bf16))
            jacc[...] += lax.dot_general(
                jnp.concatenate(values, axis=1), jnp.concatenate(picks, axis=1),
                (((1,), (1,)), ((), ())), preferred_element_type=f32,
            )
            return acc

        lax.fori_loop(first // ROWS_AT_ONCE, last // ROWS_AT_ONCE, body, 0)

    def look_up(table, labels):
        pick = jnp.concatenate([one_hot(label) for label in labels], axis=1)
        found = dot(table, pick)
        half = LEVELS * species
        results = []
        for t, label in enumerate(labels):
            level = lax.shift_right_logical(label, 7)
            column = found[:, t * LANES : (t + 1) * LANES]
            result = jnp.zeros((species, LANES), f32)
            for n in range(LEVELS):
                both = column[n * species : (n + 1) * species] + column[half + n * species : half + (n + 1) * species]
                result = result + jnp.where(level == n, both, 0.0)
            results.append(result)
        return results

    def means():
        half = LEVELS * species
        count = jnp.maximum(jacc[2 * half : 2 * half + LEVELS, :], 1.0)
        blocks = []
        for n in range(LEVELS):
            here = slice(n * species, (n + 1) * species)
            there = slice(half + n * species, half + (n + 1) * species)
            blocks.append((jacc[here, :] + jacc[there, :]) / count[n : n + 1])
        jmean[...] = jnp.concatenate(blocks, axis=0).reshape(jmean.shape)
        spread(lambda p: jmean.at[p], jrecv, SEM_J, "chan")

    def means_chan():
        arrived(jrecv, SEM_J)
        jsum[...] = jnp.sum(jrecv[...], axis=0)
        spread(lambda p: jsum, jwide, SEM_J + 1, "wide")

    def means_wide():
        arrived(jwide, SEM_J + 1)
        jpiece[...] = jnp.sum(jwide[...], axis=0)
        spread(lambda p: jpiece, jall, SEM_J + 2, "chan")

    def junction_table():
        arrived(jall, SEM_J + 2)
        table = jall[...].reshape(LEVELS * species, LANES)
        both = jnp.concatenate(split(table), axis=0)
        blocks = []
        for n in range(0, LEVELS, 2):
            found = look_up(both, [par_ref[n : n + 1, :], par_ref[n + 1 : n + 2, :]])
            for t in range(2):
                here = slice((n + t) * species, (n + t + 1) * species)
                blocks.append(coupling * (found[t] - table[here]))
        jtab[...] = jnp.concatenate(split(jnp.concatenate(blocks, axis=0)), axis=0)

    def source_rows(first, last):
        def body(i, acc):
            labels = [own_ref[pl.ds(i * ROWS_AT_ONCE + t, 1), :] for t in range(ROWS_AT_ONCE)]
            for t, found in enumerate(look_up(jtab[...], labels)):
                src[pl.ds(i * ROWS_AT_ONCE + t, species, stride=rows), :] = found
            return acc

        lax.fori_loop(first // ROWS_AT_ONCE, last // ROWS_AT_ONCE, body, 0)

    def conc_near(s):
        c = conc_ref[pl.ds(s * rows, rows), :]
        plane_l = jnp.where(wall_xl, c[:nz], conc_in[0, s])
        plane_r = jnp.where(wall_xr, c[rows - nz :], conc_in[1, s])
        line = cols_in[0, pl.ds(s + 2, 1), :], cols_in[1, pl.ds(s + 2, 1), :]
        sides = [jnp.broadcast_to(one, (cy, rows)).T for one in line]
        col_l = jnp.where(wall_yl, c, sides[0])
        col_r = jnp.where(wall_yr, c, sides[1])
        return c, neighbours(c, plane_l, plane_r, col_l, col_r, None)

    def start_species():
        loads["prev"].wait()
        arrived(conc_in.at[1], SEM_H + 6)
        arrived(conc_in.at[0], SEM_H + 7)
        for s in range(species):
            c, near_c = conc_near(s)
            flow = near_c[0]
            for k in range(1, 6):
                flow = flow + near_c[k]
            here = pl.ds(s * rows, rows)
            src[here, :] = src[here, :] + (4.0 * c - prev_ref[here, :]) + dif[s] * flow

    quarter = rows // 4
    jacc[...] = jnp.zeros_like(jacc)

    def fill(sweep, spot):
        if sweep == 0:
            if spot == 1:
                for copy in conc_halo:
                    copy.start()
            if spot == 0:
                loads["own"].wait()
            sum_rows((0, quarter, 2 * quarter)[spot], (quarter, 2 * quarter, 3 * quarter)[spot])
        elif sweep == 1:
            if spot == 0:
                sum_rows(3 * quarter, rows)
                means()
            elif spot == 1:
                means_chan()
            else:
                means_wide()
        elif sweep == 2:
            if spot == 0:
                loads["par"].wait()
                junction_table()
            elif spot == 1:
                source_rows(0, quarter)
            else:
                source_rows(quarter, 2 * quarter)
        else:
            if spot == 0:
                source_rows(2 * quarter, 3 * quarter)
            elif spot == 1:
                source_rows(3 * quarter, rows)
            else:
                start_species()

    pick_row = iota((8, 2 * cy), 0)
    pick_lane = iota((8, 2 * cy), 1)
    pick = jnp.where(
        ((pick_row == 0) & (pick_lane < cy)) | ((pick_row == 1) & (pick_lane >= cy)), 1.0, 0.0
    ).astype(bf16)
    nt = (((1,), (1,)), ((), ()))

    ring_row = iota((LANES, cx * modes), 0)
    ring_at = iota((LANES, cx * modes), 1)
    ring_pair = lax.rem((ring_row + 1) // 2, cy // 2)
    ring_keep = (ring_pair == (ring_at // modes) * nb + lax.rem(ring_at, nb))
    ring_left = lax.rem(ring_row, 2) == 1
    loads["big"].wait()

    for sweep in range(SWEEPS):
        field, near = phi_near(0)
        residual = charge[...]
        for k in range(6):
            residual = residual - faces[k] * (field - near[k])
        send1[sweep] = product(table("dt"), residual).reshape(send1.shape[1:])
        spread_fast(lambda p: send1.at[sweep, p], recv1.at[sweep], SEM_A + sweep, "chan")
        fill(sweep, 0)
        arrived(recv1.at[sweep], SEM_A + sweep)
        force = product(table("lt"), recv1[sweep].reshape(modes, cy))
        high, low = split(jnp.concatenate([force * tab_p[...], force * tab_m[...]], axis=1))
        moments = lax.dot_general(pick, high, nt, preferred_element_type=f32)
        moments = moments + lax.dot_general(pick, low, nt, preferred_element_type=f32)
        send_g[sweep] = moments[0:2]
        spread_fast(lambda p: send_g.at[sweep], recv_g.at[sweep], SEM_G + sweep, "wide")
        width = table("wy")
        inner = product_right(product_right(force, width) * tab_d[...], width)
        inner = product(table("lb"), inner)
        fill(sweep, 1)
        arrived(recv_g.at[sweep], SEM_G + sweep)
        got = recv_g[sweep]
        ends = [jnp.sum(jnp.sum(got * coef[k], axis=0), axis=0, keepdims=True) for k in range(2)]
        back_h, back_l = table("lb")
        back = back_h.astype(f32) + back_l.astype(f32)
        high, low = split(jnp.concatenate([back * ends[0], back * ends[1]], axis=1))
        outer = inner + dot(high, edge_h[...]) + dot(low, edge_h[...]) + dot(high, edge_l[...])
        span = (cx + 2) * nb
        send2[sweep, :, 0:span, :] = outer.reshape(nc, span, cy)
        long_ends = [jnp.concatenate([one] * cx, axis=1) for one in ends]
        high, low = split(jnp.where(ring_keep, jnp.where(ring_left, long_ends[0], long_ends[1]), 0.0))
        ring_h, ring_l = table("lr")
        ring = lax.dot_general(ring_h, high, nt, preferred_element_type=f32)
        ring = ring + lax.dot_general(ring_h, low, nt, preferred_element_type=f32)
        ring = ring + lax.dot_general(ring_l, high, nt, preferred_element_type=f32)
        send2[sweep, :, span : span + 1, :] = ring.reshape(nc, 1, cy)
        spread_fast(lambda p: send2.at[sweep, p], recv2.at[sweep], SEM_B + sweep, "chan")
        fill(sweep, 2)
        arrived(recv2.at[sweep], SEM_B + sweep)
        phi_e[:, 0:cy] += product(table("db"), recv2[sweep, :, 0:span, :].reshape(nc * span, cy))
        ring = recv2[sweep, :, span : span + 1, :].reshape(nc, cy)
        pieces = [pltpu.roll(ring, cy - 2 * j, 1) if j else ring for j in range(cx * nb)]
        phi_e[nz : nz + rows, cy : 2 * cy] += product(table("dr"), jnp.concatenate(pieces, axis=0))

    field, near = phi_near(None)
    out_phi[...] = field
    drops = []
    for k in range(6):
        drop = field - near[k]
        if k == 0:
            drop = jnp.where((row < nz) & wall_xl, 0.0, drop)
        elif k == 1:
            drop = jnp.where((row >= rows - nz) & wall_xr, 0.0, drop)
        elif k == 4:
            drop = jnp.where(at_first & wall_yl, 0.0, drop)
        elif k == 5:
            drop = jnp.where(at_last & wall_yr, 0.0, drop)
        drops.append(drop)
    ups = [jnp.maximum(drop, 0.0) for drop in drops]
    downs = [jnp.maximum(-drop, 0.0) for drop in drops]
    up_all = ups[0] + ups[1] + ups[2] + ups[3] + ups[4] + ups[5]
    down_all = downs[0] + downs[1] + downs[2] + downs[3] + downs[4] + downs[5]
    for k in range(6):
        faces[k] = ups[k]
        faces[6 + k] = downs[k]
    for s in range(species):
        c, near_c = conc_near(s)
        drift = val[s] * dif[s]
        plus, minus = jnp.maximum(drift, 0.0), jnp.maximum(-drift, 0.0)
        top_part = src[pl.ds(s * rows, rows), :]
        for k in range(6):
            top_part = top_part + (plus * faces[6 + k] + minus * faces[k]) * near_c[k]
        out_conc[pl.ds(s * rows, rows), :] = top_part / ((3.0 + 6.0 * dif[s]) + plus * up_all + minus * down_all)

    for copy in halo:
        copy.wait_send()
    for k in (6, 7):
        pltpu.make_async_copy(conc_in.at[0], conc_in.at[0], send_sem.at[SEM_H + k]).wait()
    for sweep in range(SWEEPS):
        left(send1.at[sweep], SEM_A + sweep, nc - 1)
        left(recv_g.at[sweep], SEM_G + sweep, nw - 1)
        left(send2.at[sweep], SEM_B + sweep, nc - 1)
    left(jmean, SEM_J, nc - 1)
    left(jwide, SEM_J + 1, nw - 1)
    left(jall, SEM_J + 2, nc - 1)


def per_device(sizes, conc_now, conc_prev, phi_prev, owner, partner, valence, diffusivity):
    nc, nw = sizes
    species, cx, nz, cy = conc_now.shape
    nb = nz // nc
    rows, modes = cx * nz, nc * cx * nb
    places, big, small = make_tables(nc, cx, nz, cy)
    ext = (cx + 2) * nz
    jrow = LEVELS * species // nc
    vmem = pl.BlockSpec(memory_space=pltpu.VMEM)
    hbm = pl.BlockSpec(memory_space=pltpu.HBM)
    sems = 3 * SWEEPS + 8 + 3
    fix = lambda x: pltpu.with_memory_space_constraint(x, pltpu.HBM)
    out_conc, out_phi = pl.pallas_call(
        functools.partial(kernel, (nc, nw, cx, nz, cy), places),
        out_shape=(
            jax.ShapeDtypeStruct((species * rows, cy), f32),
            jax.ShapeDtypeStruct((rows, cy), f32),
        ),
        in_specs=[hbm] * 9,
        out_specs=(vmem, vmem),
        scratch_shapes=[
            pltpu.SMEM((species,), jnp.int32),
            pltpu.SMEM((species,), f32),
            pltpu.VMEM((species * rows, cy), f32),
            pltpu.VMEM((species * rows, cy), f32),
            pltpu.VMEM((rows, cy), f32),
            pltpu.VMEM((rows, cy), jnp.int32),
            pltpu.VMEM((LEVELS, LANES), jnp.int32),
            pltpu.VMEM(big.shape, bf16),
            pltpu.VMEM(small.shape[1:], f32),
            pltpu.VMEM((ext, 2 * cy), f32),
            pltpu.VMEM((12, rows, cy), f32),
            pltpu.VMEM((rows, cy), f32),
            pltpu.VMEM((modes, cy), f32),
            pltpu.VMEM((modes, cy), f32),
            pltpu.VMEM((modes, cy), f32),
            pltpu.VMEM((2 * modes, cy), bf16),
            pltpu.VMEM((2 * modes, cy), bf16),
            pltpu.VMEM((2, nw, 2, modes), f32),
            pltpu.VMEM((SWEEPS, nc, cx * nb, cy), f32),
            pltpu.VMEM((SWEEPS, nc, cx * nb, cy), f32),
            pltpu.VMEM((SWEEPS, 2, modes), f32),
            pltpu.VMEM((SWEEPS, nw, 2, modes), f32),
            pltpu.VMEM((SWEEPS, nc, (cx + 2) * nb + 1, cy), f32),
            pltpu.VMEM((SWEEPS, nc, (cx + 2) * nb + 1, cy), f32),
            pltpu.VMEM((rows, cy), f32),
            pltpu.VMEM((2 * LEVELS, rows), f32),
            pltpu.VMEM((2, LEVELS, rows), f32),
            pltpu.VMEM((2, 2, nz, cy), f32),
            pltpu.VMEM((2, species, nz, cy), f32),
            pltpu.VMEM((LEVELS * (2 * species + 1), LANES), f32),
            pltpu.VMEM((nc, jrow, LANES), f32),
            pltpu.VMEM((nc, jrow, LANES), f32),
            pltpu.VMEM((jrow, LANES), f32),
            pltpu.VMEM((nw, jrow, LANES), f32),
            pltpu.VMEM((jrow, LANES), f32),
            pltpu.VMEM((nc, jrow, LANES), f32),
            pltpu.VMEM((2 * LEVELS * species, LANES), bf16),
            pltpu.VMEM((species * rows, cy), f32),
            pltpu.SemaphoreType.DMA((sems,)),
            pltpu.SemaphoreType.DMA((sems,)),
            pltpu.SemaphoreType.DMA((9,)),
        ],
        compiler_params=pltpu.CompilerParams(
            collective_id=0, has_side_effects=True, vmem_limit_bytes=48 * 1024 * 1024
        ),
        name="step",
    )(
        *[fix(x) for x in (valence, diffusivity, conc_now.reshape(species * rows, cy), conc_prev.reshape(species * rows, cy), phi_prev.reshape(rows, cy), owner.reshape(rows, cy), partner.reshape(LEVELS, LANES), jnp.asarray(big), jnp.asarray(small))]
    )
    return out_conc.reshape(conc_now.shape), out_phi.reshape(phi_prev.shape)


def solution(mesh):
    return jax.shard_map(
        functools.partial(per_device, (mesh.shape["chan"], mesh.shape["wide"])),
        mesh=mesh,
        in_specs=(
            P(None, "chan", None, "wide"),
            P(None, "chan", None, "wide"),
            P("chan", None, "wide"),
            P("chan", None, "wide"),
            P(),
            P(),
            P(),
        ),
        out_specs=(P(None, "chan", None, "wide"), P("chan", None, "wide")),
        check_vma=False,
    )
```

```python
import functools

import jax
import jax.numpy as jnp
import numpy as np
from jax import lax
from jax.experimental import pallas as pl
from jax.experimental.pallas import tpu as pltpu
from jax.sharding import PartitionSpec as P

SWEEPS = 4
charge_scale = 0.05
coupling = 2.0
conduct_ref = 1.5
LANES = 128
LEVELS = 16
ROWS_AT_ONCE = 4
MESH = pl.DeviceIdType.MESH
f32 = jnp.float32
bf16 = jnp.bfloat16


def sine_table(length):
    index = np.arange(length) + 1.0
    return np.sqrt(2.0 / (length + 1.0)) * np.sin(np.pi * np.outer(index, index) / (length + 1.0))


def eigen_values(length):
    return 2.0 - 2.0 * np.cos(np.pi * (np.arange(length) + 1.0) / (length + 1.0))


def halves(table):
    table = np.asarray(table, np.float32)
    high = table.astype(bf16)
    low = (table - high.astype(np.float32)).astype(bf16)
    return high, low


def make_tables(nc, cx, nz, cy):
    nx, nb = nc * cx, nz // nc
    qx, qz, qy = sine_table(nx), sine_table(nz), sine_table(cy)
    depth_to = np.zeros((nc, cx, nb, cx, nz))
    for x in range(cx):
        depth_to[:, x, :, x, :] = qz.reshape(nc, nb, nz)
    length_to = np.einsum("aX,bc->abXc", qx, np.eye(nb)) / conduct_ref
    length_back = np.zeros((nc, cx + 2, nb, nx, nb))
    for p in range(nc):
        for xx in range(cx + 2):
            place = cx * p + xx - 1
            if 0 <= place < nx:
                for b in range(nb):
                    length_back[p, xx, b, :, b] = qx[place]
    depth_back = np.zeros((cx + 2, nz, nc, cx + 2, nb))
    for xx in range(cx + 2):
        depth_back[xx, :, :, xx, :] = qz.reshape(nz, nc, nb)
    depth_ring = np.zeros((cx, nz, cx, nb, nc))
    for x in range(cx):
        depth_ring[x, :, x, :, :] = qz.reshape(nz, nc, nb).transpose(0, 2, 1)
    length_ring = np.zeros((nc, cx, nx, nb))
    length_ring[:] = qx.reshape(nc, cx, nx)[..., None]
    modes = nx * nb
    lam = eigen_values(nx)[:, None] + eigen_values(nz)[None, :]
    lam = lam.reshape(nx, nc, nb).transpose(1, 0, 2).reshape(nc, 1, modes)
    theta = np.arccosh(1.0 + lam / 2.0)
    big = dict(
        dt=depth_to.reshape(nc * cx * nb, cx * nz),
        lt=length_to.reshape(modes, modes),
        lb=length_back.reshape(nc * (cx + 2) * nb, modes),
        db=depth_back.reshape((cx + 2) * nz, nc * (cx + 2) * nb),
        wy=qy,
        dr=depth_ring.reshape(cx * nz, cx * nb * nc),
        lr=length_ring.reshape(nc, cx * modes),
    )
    places, parts, row = {}, [], 0
    for name, table in big.items():
        for k, half in enumerate(halves(table)):
            height = -(-half.shape[0] // 32) * 32
            block = np.zeros((height, 2 * LANES), bf16)
            block[: half.shape[0], : half.shape[1]] = half
            parts.append(block)
            places[name, k] = (row, *half.shape)
            row += height
    small = np.zeros((nc, 8, max(modes, LANES)), np.float32)
    small[:, 0, :modes] = theta[:, 0]
    small[:, 1, :modes] = lam[:, 0]
    small[:, 2, :cy] = eigen_values(cy)
    return places, np.concatenate(parts, axis=0), small


def dot(a, b):
    return jnp.dot(a, b, preferred_element_type=f32)


def split(value):
    high = value.astype(bf16)
    return high, (value - high.astype(f32)).astype(bf16)


def product(table, value):
    high, low = split(value)
    return dot(table[0], high) + dot(table[1], high) + dot(table[0], low)


def product_right(value, table):
    high, low = split(value)
    return dot(high, table[0]) + dot(high, table[1]) + dot(low, table[0])


def iota(shape, dim):
    return lax.broadcasted_iota(jnp.int32, shape, dim)


def kernel(
    cfg, places,
    val_hbm, dif_hbm, conc_hbm, prev_hbm, phi_hbm, own_hbm, par_hbm, big_hbm, small_hbm,
    out_conc, out_phi,
    val_ref, dif_ref, conc_ref, prev_ref, phi_ref, own_ref, par_ref, big, small,
    phi_e, faces, flows, beside, columns, charge, tab_p, tab_m, tab_d, edge_h, edge_l, coef,
    send1, recv1, send_g, recv_g, send2, recv2,
    sig, cols, cols_in, plane_in, conc_in,
    jacc, jmean, jrecv, jsum, jwide, jpiece, jall, jtab, src,
    send_sem, recv_sem, load_sem, known,
):
    nc, nw, cx, nz, cy = cfg
    nb = nz // nc
    rows = cx * nz
    modes = nc * cx * nb
    species = conc_ref.shape[0] // rows
    me_c = lax.axis_index("chan")
    me_w = lax.axis_index("wide")
    left_c, right_c = lax.rem(me_c + nc - 1, nc), lax.rem(me_c + 1, nc)
    left_w, right_w = lax.rem(me_w + nw - 1, nw), lax.rem(me_w + 1, nw)

    barrier = pltpu.get_barrier_semaphore()

    if nc == 32:
        order = [(dx, dy, dc) for dx in range(4) for dy in range(4) for dc in range(2)]
        hops = (0, 1, 2, 1)
        order = sorted(order[1:], key=lambda o: -(hops[o[0]] + hops[o[1]]))
        at_x = [lax.rem(me_c // 8 + d, 4) * 8 for d in range(4)]
        at_y = [lax.rem(me_c // 2 + d, 4) * 2 for d in range(4)]
        at_core = [lax.rem(me_c + d, 2) for d in range(2)]
        peers_c = [at_x[dx] + at_y[dy] + at_core[dc] for dx, dy, dc in order]
    else:
        peers_c = [lax.rem(me_c + d, nc) for d in range(1, nc)]
    peers_w = [lax.rem(me_w + d, nw) for d in sorted(range(1, nw), key=lambda d: -min(d, nw - d))]

    dx_all, dy_all = {32: (4, 4), 8: (2, 2), 4: (2, 1)}[nc]
    core = lax.rem(me_c, 2)
    chip_y = lax.rem(me_c // 2, dy_all)
    chip_x = me_c // (2 * dy_all)
    chip = lambda x, y, c: (x * dy_all + y) * 2 + c
    partner_core = chip(chip_x, chip_y, 1 - core)
    beside_chip = jnp.where(core == 0, left_c, right_c)
    row_peers = [chip(lax.rem(chip_x + d, dx_all), chip_y, core) for d in range(1, dx_all)]
    column_peers = [chip(chip_x, lax.rem(chip_y + d, dy_all), core) for d in range(1, dy_all)]
    width_peers = [left_w, right_w] if nw > 2 else [right_w]

    def tell(semaphore, axis, peers):
        for p in peers:
            pl.semaphore_signal(semaphore, inc=1, device_id={axis: p}, device_id_type=MESH)

    tell(barrier, "wide", width_peers)
    tell(barrier, "chan", [beside_chip] + row_peers + column_peers + [partner_core])

    loads = {}
    for k, (name, there, here) in enumerate([
        ("conc", conc_hbm, conc_ref), ("val", val_hbm, val_ref), ("dif", dif_hbm, dif_ref),
        ("phi", phi_hbm, phi_ref), ("small", small_hbm.at[me_c], small), ("big", big_hbm, big),
        ("own", own_hbm, own_ref), ("par", par_hbm, par_ref), ("prev", prev_hbm, prev_ref),
    ]):
        loads[name] = pltpu.make_async_copy(there, here, load_sem.at[k])
        loads[name].start()

    def table(name):
        def half(k):
            row, height, width = places[name, k]
            return big[pl.ds(row, height), pl.ds(0, width)]
        return half(0), half(1)

    lane = iota((rows, cy), 1)
    row = iota((rows, cy), 0)
    depth = lax.rem(row, nz)
    at_first, at_last = lane == 0, lane == cy - 1
    top, bottom = depth == 0, depth == nz - 1

    for name in ("val", "dif", "conc"):
        loads[name].wait()
    val = [val_ref[s].astype(f32) for s in range(species)]
    dif = [dif_ref[s] for s in range(species)]
    total = jnp.zeros((rows, cy), f32)
    part = jnp.zeros((rows, cy), f32)
    weight_all = jnp.float32(0.0)
    for s in range(species):
        c = conc_ref[pl.ds(s * rows, rows), :]
        square = val[s] * val[s]
        weight_all = weight_all + (square + 1.0) * dif[s]
        part = part + (square * dif[s]) * c * c
        total = total + val[s] * c
    sigma = 1.0 + part / jnp.full((1, 1), weight_all, f32)
    sig[...] = sigma
    loads["phi"].wait()
    phi = phi_ref[...]

    packed = jnp.zeros((rows, cy), f32)
    for k in range(species + 2):
        field = phi if k == 0 else sigma if k == 1 else conc_ref[pl.ds((k - 2) * rows, rows), :]
        packed = jnp.where(lane == k, pltpu.roll(field, k, 1) if k else field, packed)
        packed = jnp.where(lane == LEVELS + k, pltpu.roll(field, LEVELS + 1 + k, 1), packed)
    cols[...] = packed.T[: 2 * LEVELS]

    pl.semaphore_wait(barrier, 2 + len(row_peers) + len(column_peers) + len(width_peers))

    SEM_A, SEM_G, SEM_B = 0, SWEEPS, 2 * SWEEPS
    SEM_H = 3 * SWEEPS
    SEM_J = SEM_H + 8

    def remote(src, dst, k, axis, place):
        return pltpu.make_async_remote_copy(
            src_ref=src, dst_ref=dst, send_sem=send_sem.at[k], recv_sem=recv_sem.at[k],
            device_id={axis: place}, device_id_type=MESH,
        )

    halo = [
        remote(cols.at[pl.ds(0, LEVELS)], cols_in.at[1], SEM_H, "wide", left_w),
        remote(cols.at[pl.ds(LEVELS, LEVELS)], cols_in.at[0], SEM_H + 1, "wide", right_w),
        remote(sig.at[pl.ds(0, nz)], plane_in.at[1, 0], SEM_H + 2, "chan", left_c),
        remote(sig.at[pl.ds(rows - nz, nz)], plane_in.at[0, 0], SEM_H + 3, "chan", right_c),
        remote(phi_ref.at[pl.ds(0, nz)], plane_in.at[1, 1], SEM_H + 4, "chan", left_c),
        remote(phi_ref.at[pl.ds(rows - nz, nz)], plane_in.at[0, 1], SEM_H + 5, "chan", right_c),
    ]
    conc_halo = []
    for s in range(species):
        conc_halo += [
            remote(conc_ref.at[pl.ds(s * rows, nz)], conc_in.at[1, s], SEM_H + 6, "chan", left_c),
            remote(conc_ref.at[pl.ds((s + 1) * rows - nz, nz)], conc_in.at[0, s], SEM_H + 7, "chan", right_c),
        ]
    for copy in halo:
        copy.start()

    far_steps = nw // 2 - 1

    def known_w(k):
        if k > 0 and k <= far_steps:
            pl.semaphore_wait(known.at[1 + k], len(width_peers))
        if k < far_steps:
            tell(known.at[2 + k], "wide", width_peers)

    tell(known.at[0], "chan", row_peers)
    known_w(0)

    def spread(src, dst, k, axis):
        n, me = (nc, me_c) if axis == "chan" else (nw, me_w)

        def body(i, _):
            p = lax.rem(me + i, n)
            remote(src(p), dst.at[me], k, axis, p).start()
            return 0

        lax.fori_loop(1, n, body, 0)
        pltpu.make_async_copy(src(me), dst.at[me], recv_sem.at[k]).start()

    def spread_fast(src, dst, k, axis):
        peers, me = (peers_c, me_c) if axis == "chan" else (peers_w, me_w)
        for p in peers:
            remote(src(p), dst.at[me], k, axis, p).start()
        pltpu.make_async_copy(src(me), dst.at[me], recv_sem.at[k]).start()

    def arrived(dst, k):
        pltpu.make_async_copy(dst, dst, recv_sem.at[k]).wait()

    def left(ref, k, n):
        part_of = ref.at[pl.ds(0, n)]
        pltpu.make_async_copy(part_of, part_of, send_sem.at[k]).wait()

    charge[...] = charge_scale * total
    loads["small"].wait()
    theta_row = small[0:1, 0:modes]
    theta = jnp.broadcast_to(theta_row, (cy, modes)).T
    lam = jnp.broadcast_to(small[1:2, 0:modes], (cy, modes)).T
    tab_d[...] = 1.0 / (lam + small[2:3, 0:cy])
    place = iota((modes, cy), 1).astype(f32)
    power = lambda n: jnp.exp(-theta * n)
    tab_p[...] = power(place)
    tab_m[...] = power(cy - 1.0 - place)
    scale = 1.0 / (1.0 - power(2.0 * cy + 2.0))
    edge_left = (power(place + 1.0) - power(2.0 * cy + 1.0 - place)) * scale
    edge_right = (power(cy - place) - power(cy + 2.0 + place)) * scale
    for k, edge in enumerate((edge_left, edge_right)):
        high, low = split(edge)
        here = pl.ds(k * modes, modes)
        edge_h[here, pl.ds(0, cy)] = high
        edge_l[here, pl.ds(0, cy)] = low
    width1 = cy * nw + 1
    rowp = lambda n: jnp.exp(-theta_row * n)
    front = 1.0 / ((1.0 - rowp(2.0)) * (1.0 - rowp(2.0 * width1)))
    for k in range(2):
        at = (cy * me_w if k == 0 else cy * (me_w + 1) + 1).astype(f32)
        below = (1.0 - rowp(2.0 * (width1 - at))) * front
        above = (1.0 - rowp(2.0 * at)) * front
        for w in range(nw):
            lower = (w < me_w) if k == 0 else (w <= me_w)
            n_plus = jnp.where(lower, at + (cy * w + 2.0), cy * w + 2.0 - at)
            n_minus = jnp.where(lower, at - (cy * w + cy - 1.0), 2.0 * width1 - at - (cy * w + cy - 1.0))
            factor = jnp.where(lower, below, above)
            sign = jnp.where(lower, -1.0, 1.0)
            coef[k, w, 0:1, :] = sign * factor * rowp(n_plus)
            coef[k, w, 1:2, :] = -sign * factor * rowp(n_minus)

    pl.semaphore_wait(known.at[0], len(row_peers))
    tell(known.at[1], "chan", [partner_core])
    known_w(1)
    jacc[...] = jnp.zeros_like(jacc)
    faces[2] = 0.5 * (sigma + jnp.where(top, 0.0, pltpu.roll(sigma, 1, 0)))
    faces[3] = 0.5 * (sigma + jnp.where(bottom, 0.0, pltpu.roll(sigma, rows - 1, 0)))

    for copy in halo:
        copy.wait_recv()
    known_w(2)
    wall_xl, wall_xr = me_c == 0, me_c == nc - 1
    wall_yl, wall_yr = me_w == 0, me_w == nw - 1
    keep_xl, keep_xr = jnp.where(wall_xl, 0.0, 1.0), jnp.where(wall_xr, 0.0, 1.0)
    keep_yl, keep_yr = jnp.where(wall_yl, 0.0, 1.0), jnp.where(wall_yr, 0.0, 1.0)
    stacked = jnp.concatenate(
        [cols_in[0], cols_in[1], jnp.zeros((cy - 2 * LEVELS, rows), f32)], axis=0
    )
    col_in = stacked.T
    columns[...] = col_in

    def neighbours(field, plane_l, plane_r, col_l, col_r, edge):
        low = field if edge is None else jnp.zeros_like(field)
        return [
            jnp.concatenate([plane_l, field[: rows - nz]], axis=0),
            jnp.concatenate([field[nz:], plane_r], axis=0),
            jnp.where(top, low, pltpu.roll(field, 1, 0)),
            jnp.where(bottom, low, pltpu.roll(field, rows - 1, 0)),
            jnp.where(at_first, col_l, pltpu.roll(field, 1, 1)),
            jnp.where(at_last, col_r, pltpu.roll(field, cy - 1, 1)),
        ]

    near = neighbours(
        sigma, plane_in[0, 0] * keep_xl, plane_in[1, 0] * keep_xr,
        col_in[:, 1:2] * keep_yl, col_in[:, LEVELS + 1 : LEVELS + 2] * keep_yr, 0,
    )
    for k in (0, 1, 4, 5):
        faces[k] = 0.5 * (sigma + near[k])
    phi_e[0:nz, 0:cy] = plane_in[0, 1] * keep_xl
    phi_e[nz : nz + rows, 0:cy] = phi
    phi_e[nz + rows : 2 * nz + rows, 0:cy] = plane_in[1, 1] * keep_xr
    phi_e[0:nz, cy : 2 * cy] = jnp.zeros((nz, cy), f32)
    phi_e[nz + rows : 2 * nz + rows, cy : 2 * cy] = jnp.zeros((nz, cy), f32)
    zero = jnp.zeros((rows, cy), f32)
    phi_e[nz : nz + rows, cy : 2 * cy] = jnp.where(
        at_last, col_in[:, 0:1] * keep_yl, jnp.where(at_first, col_in[:, LEVELS : LEVELS + 1] * keep_yr, zero)
    )

    def phi_near(beyond):
        field = phi_e[nz : nz + rows, 0:cy]
        ring = phi_e[nz : nz + rows, cy : 2 * cy]
        low = field if beyond is None else jnp.zeros_like(field)
        return field, [
            phi_e[0:rows, 0:cy],
            phi_e[2 * nz : 2 * nz + rows, 0:cy],
            jnp.where(top, low, pltpu.roll(field, 1, 0)),
            jnp.where(bottom, low, pltpu.roll(field, rows - 1, 0)),
            pltpu.roll(jnp.where(at_last, ring, field), 1, 1),
            pltpu.roll(jnp.where(at_first, ring, field), cy - 1, 1),
        ]

    def one_hot(label):
        return jnp.where(iota((LANES, LANES), 0) == (label & (LANES - 1)), 1.0, 0.0).astype(bf16)

    def sum_rows(first, last):
        def body(i, acc):
            picks, values = [], []
            for t in range(ROWS_AT_ONCE):
                r = i * ROWS_AT_ONCE + t
                label = own_ref[pl.ds(r, 1), :]
                level = lax.shift_right_logical(label, 7)
                value = conc_ref[pl.ds(r, species, stride=rows), :]
                high = value.astype(bf16).astype(f32)
                low = value - high
                picks.append(one_hot(label))
                here = [level == n for n in range(LEVELS)]
                blocks = [jnp.where(here[n], high, 0.0) for n in range(LEVELS)]
                blocks += [jnp.where(here[n], low, 0.0) for n in range(LEVELS)]
                blocks.append(jnp.where(iota((LEVELS, LANES), 0) == level, 1.0, 0.0))
                values.append(jnp.concatenate(blocks, axis=0).astype(bf16))
            jacc[...] += lax.dot_general(
                jnp.concatenate(values, axis=1), jnp.concatenate(picks, axis=1),
                (((1,), (1,)), ((), ())), preferred_element_type=f32,
            )
            return acc

        lax.fori_loop(first // ROWS_AT_ONCE, last // ROWS_AT_ONCE, body, 0)

    def look_up(table, labels):
        pick = jnp.concatenate([one_hot(label) for label in labels], axis=1)
        found = dot(table, pick)
        half = LEVELS * species
        results = []
        for t, label in enumerate(labels):
            level = lax.shift_right_logical(label, 7)
            column = found[:, t * LANES : (t + 1) * LANES]
            result = jnp.zeros((species, LANES), f32)
            for n in range(LEVELS):
                both = column[n * species : (n + 1) * species] + column[half + n * species : half + (n + 1) * species]
                result = result + jnp.where(level == n, both, 0.0)
            results.append(result)
        return results

    def means():
        half = LEVELS * species
        count = jnp.maximum(jacc[2 * half : 2 * half + LEVELS, :], 1.0)
        blocks = []
        for n in range(LEVELS):
            here = slice(n * species, (n + 1) * species)
            there = slice(half + n * species, half + (n + 1) * species)
            blocks.append((jacc[here, :] + jacc[there, :]) / count[n : n + 1])
        jmean[...] = jnp.concatenate(blocks, axis=0).reshape(jmean.shape)
        spread(lambda p: jmean.at[p], jrecv, SEM_J, "chan")

    def means_chan():
        arrived(jrecv, SEM_J)
        jsum[...] = jnp.sum(jrecv[...], axis=0)
        spread(lambda p: jsum, jwide, SEM_J + 1, "wide")

    def means_wide():
        arrived(jwide, SEM_J + 1)
        jpiece[...] = jnp.sum(jwide[...], axis=0)
        spread(lambda p: jpiece, jall, SEM_J + 2, "chan")

    def junction_table():
        arrived(jall, SEM_J + 2)
        table = jall[...].reshape(LEVELS * species, LANES)
        both = jnp.concatenate(split(table), axis=0)
        blocks = []
        for n in range(0, LEVELS, 2):
            found = look_up(both, [par_ref[n : n + 1, :], par_ref[n + 1 : n + 2, :]])
            for t in range(2):
                here = slice((n + t) * species, (n + t + 1) * species)
                blocks.append(coupling * (found[t] - table[here]))
        jtab[...] = jnp.concatenate(split(jnp.concatenate(blocks, axis=0)), axis=0)

    def source_rows(first, last):
        def body(i, acc):
            labels = [own_ref[pl.ds(i * ROWS_AT_ONCE + t, 1), :] for t in range(ROWS_AT_ONCE)]
            for t, found in enumerate(look_up(jtab[...], labels)):
                src[pl.ds(i * ROWS_AT_ONCE + t, species, stride=rows), :] = found
            return acc

        lax.fori_loop(first // ROWS_AT_ONCE, last // ROWS_AT_ONCE, body, 0)

    def conc_near(s):
        c = conc_ref[pl.ds(s * rows, rows), :]
        plane_l = jnp.where(wall_xl, c[:nz], conc_in[0, s])
        plane_r = jnp.where(wall_xr, c[rows - nz :], conc_in[1, s])
        col_l = jnp.where(wall_yl, c, columns[:, s + 2 : s + 3])
        col_r = jnp.where(wall_yr, c, columns[:, LEVELS + s + 2 : LEVELS + s + 3])
        return c, neighbours(c, plane_l, plane_r, col_l, col_r, None)

    def start_species():
        loads["prev"].wait()
        arrived(conc_in.at[1], SEM_H + 6)
        arrived(conc_in.at[0], SEM_H + 7)
        for s in range(species):
            c, near_c = conc_near(s)
            flow = near_c[0]
            for k in range(6):
                beside[s, k] = near_c[k]
                flow = flow + near_c[k] if k else flow
            here = pl.ds(s * rows, rows)
            src[here, :] = src[here, :] + (4.0 * c - prev_ref[here, :]) + dif[s] * flow

    quarter = rows // 4

    def fill(sweep, spot):
        if sweep == 0:
            if spot == 1:
                for copy in conc_halo:
                    copy.start()
            if spot == 0:
                loads["own"].wait()
            sum_rows((0, quarter, 2 * quarter)[spot], (quarter, 2 * quarter, 3 * quarter)[spot])
        elif sweep == 1:
            if spot == 0:
                sum_rows(3 * quarter, rows)
                means()
            elif spot == 1:
                means_chan()
            else:
                means_wide()
        elif sweep == 2:
            if spot == 0:
                loads["par"].wait()
                junction_table()
            elif spot == 1:
                source_rows(0, quarter)
            else:
                source_rows(quarter, 2 * quarter)
        else:
            if spot == 0:
                source_rows(2 * quarter, 3 * quarter)
            elif spot == 1:
                source_rows(3 * quarter, rows)
            else:
                start_species()

    pick_row = iota((8, 2 * cy), 0)
    pick_lane = iota((8, 2 * cy), 1)
    pick = jnp.where(
        ((pick_row == 0) & (pick_lane < cy)) | ((pick_row == 1) & (pick_lane >= cy)), 1.0, 0.0
    ).astype(bf16)
    nt = (((1,), (1,)), ((), ()))

    ring_row = iota((LANES, cx * modes), 0)
    ring_at = iota((LANES, cx * modes), 1)
    ring_pair = lax.rem((ring_row + 1) // 2, cy // 2)
    ring_keep = (ring_pair == (ring_at // modes) * nb + lax.rem(ring_at, nb))
    ring_left = lax.rem(ring_row, 2) == 1
    loads["big"].wait()
    pl.semaphore_wait(known.at[1], 1)

    for sweep in range(SWEEPS):
        field, near = phi_near(0)
        residual = charge[...]
        for k in range(6):
            residual = residual - faces[k] * (field - near[k])
        send1[sweep] = product(table("dt"), residual).reshape(send1.shape[1:])
        spread_fast(lambda p: send1.at[sweep, p], recv1.at[sweep], SEM_A + sweep, "chan")
        fill(sweep, 0)
        arrived(recv1.at[sweep], SEM_A + sweep)
        force = product(table("lt"), recv1[sweep].reshape(modes, cy))
        high, low = split(jnp.concatenate([force * tab_p[...], force * tab_m[...]], axis=1))
        moments = lax.dot_general(pick, high, nt, preferred_element_type=f32)
        moments = moments + lax.dot_general(pick, low, nt, preferred_element_type=f32)
        send_g[sweep] = moments[0:2]
        if sweep == 0:
            for k in range(3, far_steps + 1):
                known_w(k)
        spread_fast(lambda p: send_g.at[sweep], recv_g.at[sweep], SEM_G + sweep, "wide")
        width = table("wy")
        inner = product_right(product_right(force, width) * tab_d[...], width)
        inner = product(table("lb"), inner)
        fill(sweep, 1)
        arrived(recv_g.at[sweep], SEM_G + sweep)
        got = recv_g[sweep]
        ends = [jnp.sum(jnp.sum(got * coef[k], axis=0), axis=0, keepdims=True) for k in range(2)]
        back_h, back_l = table("lb")
        back = back_h.astype(f32) + back_l.astype(f32)
        high, low = split(jnp.concatenate([back * ends[0], back * ends[1]], axis=1))
        outer = inner + dot(high, edge_h[...]) + dot(low, edge_h[...]) + dot(high, edge_l[...])
        span = (cx + 2) * nb
        send2[sweep, :, 0:span, :] = outer.reshape(nc, span, cy)
        long_ends = [jnp.concatenate([one] * cx, axis=1) for one in ends]
        high, low = split(jnp.where(ring_keep, jnp.where(ring_left, long_ends[0], long_ends[1]), 0.0))
        ring_h, ring_l = table("lr")
        ring = lax.dot_general(ring_h, high, nt, preferred_element_type=f32)
        ring = ring + lax.dot_general(ring_h, low, nt, preferred_element_type=f32)
        ring = ring + lax.dot_general(ring_l, high, nt, preferred_element_type=f32)
        send2[sweep, :, span : span + 1, :] = ring.reshape(nc, 1, cy)
        spread_fast(lambda p: send2.at[sweep, p], recv2.at[sweep], SEM_B + sweep, "chan")
        fill(sweep, 2)
        arrived(recv2.at[sweep], SEM_B + sweep)
        phi_e[:, 0:cy] += product(table("db"), recv2[sweep, :, 0:span, :].reshape(nc * span, cy))
        ring = recv2[sweep, :, span : span + 1, :].reshape(nc, cy)
        pieces = [pltpu.roll(ring, cy - 2 * j, 1) if j else ring for j in range(cx * nb)]
        phi_e[nz : nz + rows, cy : 2 * cy] += product(table("dr"), jnp.concatenate(pieces, axis=0))

    field, near = phi_near(None)
    out_phi[...] = field
    drops = []
    for k in range(6):
        drop = field - near[k]
        if k == 0:
            drop = jnp.where((row < nz) & wall_xl, 0.0, drop)
        elif k == 1:
            drop = jnp.where((row >= rows - nz) & wall_xr, 0.0, drop)
        elif k == 4:
            drop = jnp.where(at_first & wall_yl, 0.0, drop)
        elif k == 5:
            drop = jnp.where(at_last & wall_yr, 0.0, drop)
        drops.append(drop)
    outs = [jnp.zeros((rows, cy), f32)] * 2
    for k in range(6):
        up, down = jnp.maximum(drops[k], 0.0), jnp.maximum(-drops[k], 0.0)
        flows[0, k], flows[1, k] = down, up
        outs = [outs[0] + up, outs[1] + down]
    flows[0, 6], flows[1, 6] = outs
    for s in range(species):
        sign = jnp.where(val_ref[s] < 0, 1, 0)
        drift = jnp.abs(val[s] * dif[s])
        inward = flows[sign, 0] * beside[s, 0]
        for k in range(1, 6):
            inward = inward + flows[sign, k] * beside[s, k]
        here = pl.ds(s * rows, rows)
        out_conc[here, :] = (src[here, :] + drift * inward) / ((3.0 + 6.0 * dif[s]) + drift * flows[sign, 6])

    for copy in halo:
        copy.wait_send()
    for k in (6, 7):
        pltpu.make_async_copy(conc_in.at[0], conc_in.at[0], send_sem.at[SEM_H + k]).wait()
    for sweep in range(SWEEPS):
        left(send1.at[sweep], SEM_A + sweep, nc - 1)
        left(recv_g.at[sweep], SEM_G + sweep, nw - 1)
        left(send2.at[sweep], SEM_B + sweep, nc - 1)
    left(jmean, SEM_J, nc - 1)
    left(jwide, SEM_J + 1, nw - 1)
    left(jall, SEM_J + 2, nc - 1)


def per_device(sizes, conc_now, conc_prev, phi_prev, owner, partner, valence, diffusivity):
    nc, nw = sizes
    species, cx, nz, cy = conc_now.shape
    nb = nz // nc
    rows, modes = cx * nz, nc * cx * nb
    places, big, small = make_tables(nc, cx, nz, cy)
    ext = (cx + 2) * nz
    jrow = LEVELS * species // nc
    vmem = pl.BlockSpec(memory_space=pltpu.VMEM)
    hbm = pl.BlockSpec(memory_space=pltpu.HBM)
    sems = 3 * SWEEPS + 8 + 3
    fix = lambda x: pltpu.with_memory_space_constraint(x, pltpu.HBM)
    out_conc, out_phi = pl.pallas_call(
        functools.partial(kernel, (nc, nw, cx, nz, cy), places),
        out_shape=(
            jax.ShapeDtypeStruct((species * rows, cy), f32),
            jax.ShapeDtypeStruct((rows, cy), f32),
        ),
        in_specs=[hbm] * 9,
        out_specs=(vmem, vmem),
        scratch_shapes=[
            pltpu.SMEM((species,), jnp.int32),
            pltpu.SMEM((species,), f32),
            pltpu.VMEM((species * rows, cy), f32),
            pltpu.VMEM((species * rows, cy), f32),
            pltpu.VMEM((rows, cy), f32),
            pltpu.VMEM((rows, cy), jnp.int32),
            pltpu.VMEM((LEVELS, LANES), jnp.int32),
            pltpu.VMEM(big.shape, bf16),
            pltpu.VMEM(small.shape[1:], f32),
            pltpu.VMEM((ext, 2 * cy), f32),
            pltpu.VMEM((6, rows, cy), f32),
            pltpu.VMEM((2, 7, rows, cy), f32),
            pltpu.VMEM((species, 6, rows, cy), f32),
            pltpu.VMEM((rows, cy), f32),
            pltpu.VMEM((rows, cy), f32),
            pltpu.VMEM((modes, cy), f32),
            pltpu.VMEM((modes, cy), f32),
            pltpu.VMEM((modes, cy), f32),
            pltpu.VMEM((2 * modes, cy), bf16),
            pltpu.VMEM((2 * modes, cy), bf16),
            pltpu.VMEM((2, nw, 2, modes), f32),
            pltpu.VMEM((SWEEPS, nc, cx * nb, cy), f32),
            pltpu.VMEM((SWEEPS, nc, cx * nb, cy), f32),
            pltpu.VMEM((SWEEPS, 2, modes), f32),
            pltpu.VMEM((SWEEPS, nw, 2, modes), f32),
            pltpu.VMEM((SWEEPS, nc, (cx + 2) * nb + 1, cy), f32),
            pltpu.VMEM((SWEEPS, nc, (cx + 2) * nb + 1, cy), f32),
            pltpu.VMEM((rows, cy), f32),
            pltpu.VMEM((2 * LEVELS, rows), f32),
            pltpu.VMEM((2, LEVELS, rows), f32),
            pltpu.VMEM((2, 2, nz, cy), f32),
            pltpu.VMEM((2, species, nz, cy), f32),
            pltpu.VMEM((LEVELS * (2 * species + 1), LANES), f32),
            pltpu.VMEM((nc, jrow, LANES), f32),
            pltpu.VMEM((nc, jrow, LANES), f32),
            pltpu.VMEM((jrow, LANES), f32),
            pltpu.VMEM((nw, jrow, LANES), f32),
            pltpu.VMEM((jrow, LANES), f32),
            pltpu.VMEM((nc, jrow, LANES), f32),
            pltpu.VMEM((2 * LEVELS * species, LANES), bf16),
            pltpu.VMEM((species * rows, cy), f32),
            pltpu.SemaphoreType.DMA((sems,)),
            pltpu.SemaphoreType.DMA((sems,)),
            pltpu.SemaphoreType.DMA((9,)),
            pltpu.SemaphoreType.REGULAR((2 + max(nw // 2 - 1, 1),)),
        ],
        compiler_params=pltpu.CompilerParams(
            collective_id=0, has_side_effects=True, vmem_limit_bytes=48 * 1024 * 1024
        ),
        name="step",
    )(
        *[fix(x) for x in (valence, diffusivity, conc_now.reshape(species * rows, cy), conc_prev.reshape(species * rows, cy), phi_prev.reshape(rows, cy), owner.reshape(rows, cy), partner.reshape(LEVELS, LANES), jnp.asarray(big), jnp.asarray(small))]
    )
    return out_conc.reshape(conc_now.shape), out_phi.reshape(phi_prev.shape)


def solution(mesh):
    return jax.shard_map(
        functools.partial(per_device, (mesh.shape["chan"], mesh.shape["wide"])),
        mesh=mesh,
        in_specs=(
            P(None, "chan", None, "wide"),
            P(None, "chan", None, "wide"),
            P("chan", None, "wide"),
            P("chan", None, "wide"),
            P(),
            P(),
            P(),
        ),
        out_specs=(P(None, "chan", None, "wide"), P("chan", None, "wide")),
        check_vma=False,
    )
```

```python
import functools

import jax
import jax.numpy as jnp
import numpy as np
from jax import lax
from jax.experimental import pallas as pl
from jax.experimental.pallas import tpu as pltpu
from jax.sharding import PartitionSpec as P

SWEEPS = 4
charge_scale = 0.05
coupling = 2.0
conduct_ref = 1.5
LANES = 128
LEVELS = 16
ROWS_AT_ONCE = 4
MESH = pl.DeviceIdType.MESH
f32 = jnp.float32
bf16 = jnp.bfloat16


def sine_table(length):
    index = np.arange(length) + 1.0
    return np.sqrt(2.0 / (length + 1.0)) * np.sin(np.pi * np.outer(index, index) / (length + 1.0))


def eigen_values(length):
    return 2.0 - 2.0 * np.cos(np.pi * (np.arange(length) + 1.0) / (length + 1.0))


def halves(table):
    table = np.asarray(table, np.float32)
    high = table.astype(bf16)
    low = (table - high.astype(np.float32)).astype(bf16)
    return high, low


def make_tables(nc, cx, nz, cy):
    nx, nb = nc * cx, nz // nc
    qx, qz, qy = sine_table(nx), sine_table(nz), sine_table(cy)
    depth_to = np.zeros((nc, cx, nb, cx, nz))
    for x in range(cx):
        depth_to[:, x, :, x, :] = qz.reshape(nc, nb, nz)
    length_to = np.einsum("aX,bc->abXc", qx, np.eye(nb)) / conduct_ref
    length_back = np.zeros((nc, cx + 2, nb, nx, nb))
    for p in range(nc):
        for xx in range(cx + 2):
            place = cx * p + xx - 1
            if 0 <= place < nx:
                for b in range(nb):
                    length_back[p, xx, b, :, b] = qx[place]
    depth_back = np.zeros((cx + 2, nz, nc, cx + 2, nb))
    for xx in range(cx + 2):
        depth_back[xx, :, :, xx, :] = qz.reshape(nz, nc, nb)
    depth_ring = np.zeros((cx, nz, cx, nb, nc))
    for x in range(cx):
        depth_ring[x, :, x, :, :] = qz.reshape(nz, nc, nb).transpose(0, 2, 1)
    length_ring = np.zeros((cx, nc, nx, nb))
    length_ring[:] = qx.reshape(nc, cx, nx).transpose(1, 0, 2)[..., None]
    lane_pick = np.zeros((cx, 2, nx, nb, cy))
    for x in range(cx):
        for b in range(nb):
            lane_pick[x, 0, :, b, (2 * (x * nb + b) - 1) % cy] = 1.0
            lane_pick[x, 1, :, b, 2 * (x * nb + b)] = 1.0
    modes = nx * nb
    lam = eigen_values(nx)[:, None] + eigen_values(nz)[None, :]
    lam = lam.reshape(nx, nc, nb).transpose(1, 0, 2).reshape(nc, 1, modes)
    theta = np.arccosh(1.0 + lam / 2.0)
    big = dict(
        dt=depth_to.reshape(nc * cx * nb, cx * nz),
        lt=length_to.reshape(modes, modes),
        lb=length_back.reshape(nc * (cx + 2) * nb, modes),
        db=depth_back.reshape((cx + 2) * nz, nc * (cx + 2) * nb),
        wy=qy,
        dr=depth_ring.reshape(cx * nz, cx * nb * nc),
        lr=length_ring.reshape(cx * nc, modes),
        lp=lane_pick.reshape(cx * 2 * modes, cy),
    )
    places, parts, row = {}, [], 0
    for name, table in big.items():
        pair = halves(table)
        if name in ("dt", "lt", "lb", "dr"):
            pair = (np.concatenate(pair, axis=1),)
        if name == "lr":
            pair = (np.concatenate(pair, axis=0),)
        if name == "lp":
            pair = pair[:1]
        for k, half in enumerate(pair):
            height = -(-half.shape[0] // 32) * 32
            block = np.zeros((height, 2 * LANES), bf16)
            block[: half.shape[0], : half.shape[1]] = half
            parts.append(block)
            places[name, k] = (row, *half.shape)
            row += height
    small = np.zeros((nc, 8, max(modes, LANES)), np.float32)
    small[:, 0, :modes] = theta[:, 0]
    small[:, 1, :modes] = lam[:, 0]
    small[:, 2, :cy] = eigen_values(cy)
    return places, np.concatenate(parts, axis=0), small


def dot(a, b):
    return jnp.dot(a, b, preferred_element_type=f32)


def split(value):
    high = value.astype(bf16)
    return high, (value - high.astype(f32)).astype(bf16)


def product(table, value):
    high, low = split(value)
    width = value.shape[1]
    found = dot(table[0], jnp.concatenate([high, low], axis=1))
    return found[:, :width] + found[:, width:] + dot(table[1], high)


def product_right(value, table):
    high, low = split(value)
    return dot(high, table[0]) + dot(high, table[1]) + dot(low, table[0])


def iota(shape, dim):
    return lax.broadcasted_iota(jnp.int32, shape, dim)


def kernel(
    cfg, places,
    val_hbm, dif_hbm, conc_hbm, prev_hbm, phi_hbm, own_hbm, par_hbm, big_hbm, small_hbm,
    out_conc, out_phi,
    val_ref, dif_ref, conc_ref, prev_ref, phi_ref, own_ref, par_ref, big, small,
    phi_e, faces, flows, beside, columns, charge, decay_h, decay_l, length_t, tab_d, edges, coef,
    send1, recv1, send_g, recv_g, send2, recv2,
    sig, cols, cols_in, plane_in, conc_in,
    jacc, jmean, jrecv, jsum, jwide, jpiece, jall, jtab, src,
    send_sem, recv_sem, load_sem, known,
):
    nc, nw, cx, nz, cy = cfg
    nb = nz // nc
    rows = cx * nz
    modes = nc * cx * nb
    species = conc_ref.shape[0] // rows
    me_c = lax.axis_index("chan")
    me_w = lax.axis_index("wide")
    left_c, right_c = lax.rem(me_c + nc - 1, nc), lax.rem(me_c + 1, nc)
    left_w, right_w = lax.rem(me_w + nw - 1, nw), lax.rem(me_w + 1, nw)

    barrier = pltpu.get_barrier_semaphore()

    if nc == 32:
        order = [(dx, dy, dc) for dx in range(4) for dy in range(4) for dc in range(2)]
        hops = (0, 1, 2, 1)
        order = sorted(order[1:], key=lambda o: -(hops[o[0]] + hops[o[1]]))
        at_x = [lax.rem(me_c // 8 + d, 4) * 8 for d in range(4)]
        at_y = [lax.rem(me_c // 2 + d, 4) * 2 for d in range(4)]
        at_core = [lax.rem(me_c + d, 2) for d in range(2)]
        peers_c = [at_x[dx] + at_y[dy] + at_core[dc] for dx, dy, dc in order]
    else:
        peers_c = [lax.rem(me_c + d, nc) for d in range(1, nc)]
    peers_w = [lax.rem(me_w + d, nw) for d in sorted(range(1, nw), key=lambda d: -min(d, nw - d))]

    dx_all, dy_all = {32: (4, 4), 8: (2, 2), 4: (2, 1)}[nc]
    core = lax.rem(me_c, 2)
    chip_y = lax.rem(me_c // 2, dy_all)
    chip_x = me_c // (2 * dy_all)
    chip = lambda x, y, c: (x * dy_all + y) * 2 + c
    partner_core = chip(chip_x, chip_y, 1 - core)
    beside_chip = jnp.where(core == 0, left_c, right_c)
    row_peers = [chip(lax.rem(chip_x + d, dx_all), chip_y, core) for d in range(1, dx_all)]
    column_peers = [chip(chip_x, lax.rem(chip_y + d, dy_all), core) for d in range(1, dy_all)]
    width_peers = [left_w, right_w] if nw > 2 else [right_w]

    def tell(semaphore, axis, peers):
        for p in peers:
            pl.semaphore_signal(semaphore, inc=1, device_id={axis: p}, device_id_type=MESH)

    tell(barrier, "wide", width_peers)
    tell(barrier, "chan", [beside_chip] + row_peers + column_peers + [partner_core])

    loads = {}
    for k, (name, there, here) in enumerate([
        ("conc", conc_hbm, conc_ref), ("val", val_hbm, val_ref), ("dif", dif_hbm, dif_ref),
        ("phi", phi_hbm, phi_ref), ("small", small_hbm.at[me_c], small), ("big", big_hbm, big),
        ("own", own_hbm, own_ref), ("par", par_hbm, par_ref), ("prev", prev_hbm, prev_ref),
    ]):
        loads[name] = pltpu.make_async_copy(there, here, load_sem.at[k])
        loads[name].start()

    def table(name):
        def half(k):
            row, height, width = places[name, k]
            return big[pl.ds(row, height), pl.ds(0, width)]
        return half(0), half(1)

    def twin(name):
        row, height, width = places[name, 0]
        return big[pl.ds(row, height), pl.ds(0, width)]

    def product_twin(name, value):
        both = twin(name)
        high, low = split(value)
        width = value.shape[1]
        value = jnp.concatenate(
            [jnp.concatenate([high, high], axis=0), jnp.concatenate([low, jnp.zeros_like(low)], axis=0)], axis=1
        )
        found = dot(both, value)
        return found[:, :width] + found[:, width:]

    lane = iota((rows, cy), 1)
    row = iota((rows, cy), 0)
    depth = lax.rem(row, nz)
    at_first, at_last = lane == 0, lane == cy - 1
    top, bottom = depth == 0, depth == nz - 1

    for name in ("val", "dif", "conc"):
        loads[name].wait()
    val = [val_ref[s].astype(f32) for s in range(species)]
    dif = [dif_ref[s] for s in range(species)]
    total = jnp.zeros((rows, cy), f32)
    part = jnp.zeros((rows, cy), f32)
    weight_all = jnp.float32(0.0)
    for s in range(species):
        c = conc_ref[pl.ds(s * rows, rows), :]
        square = val[s] * val[s]
        weight_all = weight_all + (square + 1.0) * dif[s]
        part = part + (square * dif[s]) * c * c
        total = total + val[s] * c
    sigma = 1.0 + part / jnp.full((1, 1), weight_all, f32)
    sig[...] = sigma
    loads["phi"].wait()
    phi = phi_ref[...]

    packed = jnp.zeros((rows, cy), f32)
    for k in range(species + 2):
        field = phi if k == 0 else sigma if k == 1 else conc_ref[pl.ds((k - 2) * rows, rows), :]
        packed = jnp.where(lane == k, pltpu.roll(field, k, 1) if k else field, packed)
        packed = jnp.where(lane == LEVELS + k, pltpu.roll(field, LEVELS + 1 + k, 1), packed)
    cols[...] = packed.T[: 2 * LEVELS]

    pl.semaphore_wait(barrier, 2 + len(row_peers) + len(column_peers) + len(width_peers))

    SEM_A, SEM_G, SEM_B = 0, SWEEPS, 2 * SWEEPS
    SEM_H = 3 * SWEEPS
    SEM_J = SEM_H + 8

    def remote(src, dst, k, axis, place):
        return pltpu.make_async_remote_copy(
            src_ref=src, dst_ref=dst, send_sem=send_sem.at[k], recv_sem=recv_sem.at[k],
            device_id={axis: place}, device_id_type=MESH,
        )

    halo = [
        remote(cols.at[pl.ds(0, LEVELS)], cols_in.at[1], SEM_H, "wide", left_w),
        remote(cols.at[pl.ds(LEVELS, LEVELS)], cols_in.at[0], SEM_H + 1, "wide", right_w),
        remote(sig.at[pl.ds(0, nz)], plane_in.at[1, 0], SEM_H + 2, "chan", left_c),
        remote(sig.at[pl.ds(rows - nz, nz)], plane_in.at[0, 0], SEM_H + 3, "chan", right_c),
        remote(phi_ref.at[pl.ds(0, nz)], plane_in.at[1, 1], SEM_H + 4, "chan", left_c),
        remote(phi_ref.at[pl.ds(rows - nz, nz)], plane_in.at[0, 1], SEM_H + 5, "chan", right_c),
    ]
    conc_halo = []
    for s in range(species):
        conc_halo += [
            remote(conc_ref.at[pl.ds(s * rows, nz)], conc_in.at[1, s], SEM_H + 6, "chan", left_c),
            remote(conc_ref.at[pl.ds((s + 1) * rows - nz, nz)], conc_in.at[0, s], SEM_H + 7, "chan", right_c),
        ]
    for copy in halo:
        copy.start()

    far_steps = nw // 2 - 1

    def known_w(k):
        if k > 0 and k <= far_steps:
            pl.semaphore_wait(known.at[1 + k], len(width_peers))
        if k < far_steps:
            tell(known.at[2 + k], "wide", width_peers)

    tell(known.at[0], "chan", row_peers)
    known_w(0)

    def spread(src, dst, k, axis):
        n, me = (nc, me_c) if axis == "chan" else (nw, me_w)

        def body(i, _):
            p = lax.rem(me + i, n)
            remote(src(p), dst.at[me], k, axis, p).start()
            return 0

        lax.fori_loop(1, n, body, 0)
        pltpu.make_async_copy(src(me), dst.at[me], recv_sem.at[k]).start()

    def spread_fast(src, dst, k, axis):
        peers, me = (peers_c, me_c) if axis == "chan" else (peers_w, me_w)
        for p in peers:
            remote(src(p), dst.at[me], k, axis, p).start()
        pltpu.make_async_copy(src(me), dst.at[me], recv_sem.at[k]).start()

    def arrived(dst, k):
        pltpu.make_async_copy(dst, dst, recv_sem.at[k]).wait()

    def left(ref, k, n):
        part_of = ref.at[pl.ds(0, n)]
        pltpu.make_async_copy(part_of, part_of, send_sem.at[k]).wait()

    charge[...] = charge_scale * total
    loads["small"].wait()
    theta_row = small[0:1, 0:modes]
    theta = jnp.broadcast_to(theta_row, (cy, modes)).T
    lam = jnp.broadcast_to(small[1:2, 0:modes], (cy, modes)).T
    tab_d[...] = 1.0 / (lam + small[2:3, 0:cy])
    place = iota((modes, cy), 1).astype(f32)
    power = lambda n: jnp.exp(-theta * n)
    down = iota((cy, modes), 0).astype(f32)
    high, low = split(jnp.concatenate([jnp.exp(-theta_row * down), jnp.exp(-theta_row * (cy - 1.0 - down))], axis=1))
    decay_h[...] = jnp.concatenate([high, high], axis=0)
    decay_l[...] = low
    scale = 1.0 / (1.0 - power(2.0 * cy + 2.0))
    edge_left = (power(place + 1.0) - power(2.0 * cy + 1.0 - place)) * scale
    edge_right = (power(cy - place) - power(cy + 2.0 + place)) * scale
    for k, edge in enumerate((edge_left, edge_right)):
        high, low = split(edge)
        here = pl.ds(k * modes, modes)
        edges[here, 0:cy] = high
        edges[here, cy : 2 * cy] = low
    width1 = cy * nw + 1
    rowp = lambda n: jnp.exp(-theta_row * n)
    front = 1.0 / ((1.0 - rowp(2.0)) * (1.0 - rowp(2.0 * width1)))
    for k in range(2):
        at = (cy * me_w if k == 0 else cy * (me_w + 1) + 1).astype(f32)
        below = (1.0 - rowp(2.0 * (width1 - at))) * front
        above = (1.0 - rowp(2.0 * at)) * front
        for w in range(nw):
            lower = (w < me_w) if k == 0 else (w <= me_w)
            n_plus = jnp.where(lower, at + (cy * w + 2.0), cy * w + 2.0 - at)
            n_minus = jnp.where(lower, at - (cy * w + cy - 1.0), 2.0 * width1 - at - (cy * w + cy - 1.0))
            factor = jnp.where(lower, below, above)
            sign = jnp.where(lower, -1.0, 1.0)
            coef[k, w, 0:1, :] = sign * factor * rowp(n_plus)
            coef[k, w, 1:2, :] = -sign * factor * rowp(n_minus)

    pl.semaphore_wait(known.at[0], len(row_peers))
    tell(known.at[1], "chan", [partner_core])
    known_w(1)
    jacc[...] = jnp.zeros_like(jacc)
    faces[2] = 0.5 * (sigma + jnp.where(top, 0.0, pltpu.roll(sigma, 1, 0)))
    faces[3] = 0.5 * (sigma + jnp.where(bottom, 0.0, pltpu.roll(sigma, rows - 1, 0)))

    loads["big"].wait()
    length = twin("lt")
    length = (length[:, :modes].astype(f32) + length[:, modes:].astype(f32)).T
    length_t[...] = jnp.concatenate([length, length], axis=1)

    for copy in halo:
        copy.wait_recv()
    known_w(2)
    wall_xl, wall_xr = me_c == 0, me_c == nc - 1
    wall_yl, wall_yr = me_w == 0, me_w == nw - 1
    keep_xl, keep_xr = jnp.where(wall_xl, 0.0, 1.0), jnp.where(wall_xr, 0.0, 1.0)
    keep_yl, keep_yr = jnp.where(wall_yl, 0.0, 1.0), jnp.where(wall_yr, 0.0, 1.0)
    stacked = jnp.concatenate(
        [cols_in[0], cols_in[1], jnp.zeros((cy - 2 * LEVELS, rows), f32)], axis=0
    )
    col_in = stacked.T
    columns[...] = col_in

    def neighbours(field, plane_l, plane_r, col_l, col_r, edge):
        low = field if edge is None else jnp.zeros_like(field)
        return [
            jnp.concatenate([plane_l, field[: rows - nz]], axis=0),
            jnp.concatenate([field[nz:], plane_r], axis=0),
            jnp.where(top, low, pltpu.roll(field, 1, 0)),
            jnp.where(bottom, low, pltpu.roll(field, rows - 1, 0)),
            jnp.where(at_first, col_l, pltpu.roll(field, 1, 1)),
            jnp.where(at_last, col_r, pltpu.roll(field, cy - 1, 1)),
        ]

    near = neighbours(
        sigma, plane_in[0, 0] * keep_xl, plane_in[1, 0] * keep_xr,
        col_in[:, 1:2] * keep_yl, col_in[:, LEVELS + 1 : LEVELS + 2] * keep_yr, 0,
    )
    for k in (0, 1, 4, 5):
        faces[k] = 0.5 * (sigma + near[k])
    phi_e[0:nz, 0:cy] = plane_in[0, 1] * keep_xl
    phi_e[nz : nz + rows, 0:cy] = phi
    phi_e[nz + rows : 2 * nz + rows, 0:cy] = plane_in[1, 1] * keep_xr
    phi_e[0:nz, cy : 2 * cy] = jnp.zeros((nz, cy), f32)
    phi_e[nz + rows : 2 * nz + rows, cy : 2 * cy] = jnp.zeros((nz, cy), f32)
    zero = jnp.zeros((rows, cy), f32)
    phi_e[nz : nz + rows, cy : 2 * cy] = jnp.where(
        at_last, col_in[:, 0:1] * keep_yl, jnp.where(at_first, col_in[:, LEVELS : LEVELS + 1] * keep_yr, zero)
    )

    def phi_near(beyond):
        field = phi_e[nz : nz + rows, 0:cy]
        ring = phi_e[nz : nz + rows, cy : 2 * cy]
        low = field if beyond is None else jnp.zeros_like(field)
        return field, [
            phi_e[0:rows, 0:cy],
            phi_e[2 * nz : 2 * nz + rows, 0:cy],
            jnp.where(top, low, pltpu.roll(field, 1, 0)),
            jnp.where(bottom, low, pltpu.roll(field, rows - 1, 0)),
            pltpu.roll(jnp.where(at_last, ring, field), 1, 1),
            pltpu.roll(jnp.where(at_first, ring, field), cy - 1, 1),
        ]

    def one_hot(label):
        return jnp.where(iota((LANES, LANES), 0) == (label & (LANES - 1)), 1.0, 0.0).astype(bf16)

    def sum_rows(first, last):
        def body(i, acc):
            picks, values = [], []
            for t in range(ROWS_AT_ONCE):
                r = i * ROWS_AT_ONCE + t
                label = own_ref[pl.ds(r, 1), :]
                level = lax.shift_right_logical(label, 7)
                value = conc_ref[pl.ds(r, species, stride=rows), :]
                high = value.astype(bf16).astype(f32)
                low = value - high
                picks.append(one_hot(label))
                here = [level == n for n in range(LEVELS)]
                blocks = [jnp.where(here[n], high, 0.0) for n in range(LEVELS)]
                blocks += [jnp.where(here[n], low, 0.0) for n in range(LEVELS)]
                blocks.append(jnp.where(iota((LEVELS, LANES), 0) == level, 1.0, 0.0))
                values.append(jnp.concatenate(blocks, axis=0).astype(bf16))
            jacc[...] += lax.dot_general(
                jnp.concatenate(values, axis=1), jnp.concatenate(picks, axis=1),
                (((1,), (1,)), ((), ())), preferred_element_type=f32,
            )
            return acc

        lax.fori_loop(first // ROWS_AT_ONCE, last // ROWS_AT_ONCE, body, 0)

    def look_up(table, labels):
        pick = jnp.concatenate([one_hot(label) for label in labels], axis=1)
        found = dot(table, pick)
        half = LEVELS * species
        results = []
        for t, label in enumerate(labels):
            level = lax.shift_right_logical(label, 7)
            column = found[:, t * LANES : (t + 1) * LANES]
            result = jnp.zeros((species, LANES), f32)
            for n in range(LEVELS):
                both = column[n * species : (n + 1) * species] + column[half + n * species : half + (n + 1) * species]
                result = result + jnp.where(level == n, both, 0.0)
            results.append(result)
        return results

    def means():
        half = LEVELS * species
        count = jnp.maximum(jacc[2 * half : 2 * half + LEVELS, :], 1.0)
        blocks = []
        for n in range(LEVELS):
            here = slice(n * species, (n + 1) * species)
            there = slice(half + n * species, half + (n + 1) * species)
            blocks.append((jacc[here, :] + jacc[there, :]) / count[n : n + 1])
        jmean[...] = jnp.concatenate(blocks, axis=0).reshape(jmean.shape)
        spread(lambda p: jmean.at[p], jrecv, SEM_J, "chan")

    def means_chan():
        arrived(jrecv, SEM_J)
        jsum[...] = jnp.sum(jrecv[...], axis=0)
        spread(lambda p: jsum, jwide, SEM_J + 1, "wide")

    def means_wide():
        arrived(jwide, SEM_J + 1)
        jpiece[...] = jnp.sum(jwide[...], axis=0)
        spread(lambda p: jpiece, jall, SEM_J + 2, "chan")

    def junction_table():
        arrived(jall, SEM_J + 2)
        table = jall[...].reshape(LEVELS * species, LANES)
        both = jnp.concatenate(split(table), axis=0)
        blocks = []
        for n in range(0, LEVELS, 2):
            found = look_up(both, [par_ref[n : n + 1, :], par_ref[n + 1 : n + 2, :]])
            for t in range(2):
                here = slice((n + t) * species, (n + t + 1) * species)
                blocks.append(coupling * (found[t] - table[here]))
        jtab[...] = jnp.concatenate(split(jnp.concatenate(blocks, axis=0)), axis=0)

    def source_rows(first, last):
        def body(i, acc):
            labels = [own_ref[pl.ds(i * ROWS_AT_ONCE + t, 1), :] for t in range(ROWS_AT_ONCE)]
            for t, found in enumerate(look_up(jtab[...], labels)):
                src[pl.ds(i * ROWS_AT_ONCE + t, species, stride=rows), :] = found
            return acc

        lax.fori_loop(first // ROWS_AT_ONCE, last // ROWS_AT_ONCE, body, 0)

    def conc_near(s):
        c = conc_ref[pl.ds(s * rows, rows), :]
        plane_l = jnp.where(wall_xl, c[:nz], conc_in[0, s])
        plane_r = jnp.where(wall_xr, c[rows - nz :], conc_in[1, s])
        col_l = jnp.where(wall_yl, c, columns[:, s + 2 : s + 3])
        col_r = jnp.where(wall_yr, c, columns[:, LEVELS + s + 2 : LEVELS + s + 3])
        return c, neighbours(c, plane_l, plane_r, col_l, col_r, None)

    def start_species():
        loads["prev"].wait()
        arrived(conc_in.at[1], SEM_H + 6)
        arrived(conc_in.at[0], SEM_H + 7)
        for s in range(species):
            c, near_c = conc_near(s)
            flow = near_c[0]
            for k in range(6):
                beside[s, k] = near_c[k]
                flow = flow + near_c[k] if k else flow
            here = pl.ds(s * rows, rows)
            src[here, :] = src[here, :] + (4.0 * c - prev_ref[here, :]) + dif[s] * flow

    quarter = rows // 4

    def fill(sweep, spot):
        if sweep == 0:
            if spot == 1:
                for copy in conc_halo:
                    copy.start()
            if spot == 0:
                loads["own"].wait()
            sum_rows((0, quarter, 2 * quarter)[spot], (quarter, 2 * quarter, 3 * quarter)[spot])
        elif sweep == 1:
            if spot == 0:
                sum_rows(3 * quarter, rows)
                means()
            elif spot == 1:
                means_chan()
            else:
                means_wide()
        elif sweep == 2:
            if spot == 0:
                loads["par"].wait()
                junction_table()
            elif spot == 1:
                source_rows(0, quarter)
            else:
                source_rows(quarter, 2 * quarter)
        else:
            if spot == 0:
                source_rows(2 * quarter, 3 * quarter)
            elif spot == 1:
                source_rows(3 * quarter, rows)
            else:
                start_species()


    pl.semaphore_wait(known.at[1], 1)

    for sweep in range(SWEEPS):
        field, near = phi_near(0)
        residual = charge[...]
        for k in range(6):
            residual = residual - faces[k] * (field - near[k])
        send1[sweep] = product_twin("dt", residual).reshape(send1.shape[1:])
        spread_fast(lambda p: send1.at[sweep, p], recv1.at[sweep], SEM_A + sweep, "chan")
        fill(sweep, 0)
        arrived(recv1.at[sweep], SEM_A + sweep)
        arrival = recv1[sweep].reshape(modes, cy)
        high, low = split(arrival)
        decayed = dot(jnp.concatenate([high, low], axis=1), decay_h[...]) + dot(high, decay_l[...])
        moments = jnp.sum(decayed * length_t[...], axis=0, keepdims=True)
        send_g[sweep, 0:1, :] = moments[:, :modes]
        send_g[sweep, 1:2, :] = moments[:, modes:]
        if sweep == 0:
            for k in range(3, far_steps + 1):
                known_w(k)
        spread_fast(lambda p: send_g.at[sweep], recv_g.at[sweep], SEM_G + sweep, "wide")
        force = product_twin("lt", arrival)
        width = table("wy")
        inner = product_right(product_right(force, width) * tab_d[...], width)
        inner = product_twin("lb", inner)
        fill(sweep, 1)
        arrived(recv_g.at[sweep], SEM_G + sweep)
        got = recv_g[sweep]
        ends = [jnp.sum(jnp.sum(got * coef[k], axis=0), axis=0, keepdims=True) for k in range(2)]
        back = twin("lb")
        back = back[:, :modes].astype(f32) + back[:, modes:].astype(f32)
        high, low = split(jnp.concatenate([back * ends[0], back * ends[1]], axis=1))
        outer = dot(high, edges[...])
        outer = inner + outer[:, :cy] + outer[:, cy:] + dot(low, edges[:, 0:cy])
        span = (cx + 2) * nb
        send2[sweep, :, 0:span, :] = outer.reshape(nc, span, cy)
        lines = twin("lr")
        lines = lines[: nc * cx].astype(f32) + lines[nc * cx :].astype(f32)
        lines = jnp.concatenate([lines[x * nc : (x + 1) * nc] * end for x in range(cx) for end in ends], axis=1)
        high, low = split(lines)
        ring = dot(high, twin("lp")) + dot(low, twin("lp"))
        send2[sweep, :, span : span + 1, :] = ring.reshape(nc, 1, cy)
        spread_fast(lambda p: send2.at[sweep, p], recv2.at[sweep], SEM_B + sweep, "chan")
        fill(sweep, 2)
        arrived(recv2.at[sweep], SEM_B + sweep)
        phi_e[:, 0:cy] += product(table("db"), recv2[sweep, :, 0:span, :].reshape(nc * span, cy))
        ring = recv2[sweep, :, span : span + 1, :].reshape(nc, cy)
        pieces = [pltpu.roll(ring, cy - 2 * j, 1) if j else ring for j in range(cx * nb)]
        phi_e[nz : nz + rows, cy : 2 * cy] += product_twin("dr", jnp.concatenate(pieces, axis=0))

    field, near = phi_near(None)
    out_phi[...] = field
    drops = []
    for k in range(6):
        drop = field - near[k]
        if k == 0:
            drop = jnp.where((row < nz) & wall_xl, 0.0, drop)
        elif k == 1:
            drop = jnp.where((row >= rows - nz) & wall_xr, 0.0, drop)
        elif k == 4:
            drop = jnp.where(at_first & wall_yl, 0.0, drop)
        elif k == 5:
            drop = jnp.where(at_last & wall_yr, 0.0, drop)
        drops.append(drop)
    outs = [jnp.zeros((rows, cy), f32)] * 2
    for k in range(6):
        up, down = jnp.maximum(drops[k], 0.0), jnp.maximum(-drops[k], 0.0)
        flows[0, k], flows[1, k] = down, up
        outs = [outs[0] + up, outs[1] + down]
    flows[0, 6], flows[1, 6] = outs
    for s in range(species):
        sign = jnp.where(val_ref[s] < 0, 1, 0)
        drift = jnp.abs(val[s] * dif[s])
        inward = flows[sign, 0] * beside[s, 0]
        for k in range(1, 6):
            inward = inward + flows[sign, k] * beside[s, k]
        here = pl.ds(s * rows, rows)
        out_conc[here, :] = (src[here, :] + drift * inward) / ((3.0 + 6.0 * dif[s]) + drift * flows[sign, 6])

    for copy in halo:
        copy.wait_send()
    for k in (6, 7):
        pltpu.make_async_copy(conc_in.at[0], conc_in.at[0], send_sem.at[SEM_H + k]).wait()
    for sweep in range(SWEEPS):
        left(send1.at[sweep], SEM_A + sweep, nc - 1)
        left(recv_g.at[sweep], SEM_G + sweep, nw - 1)
        left(send2.at[sweep], SEM_B + sweep, nc - 1)
    left(jmean, SEM_J, nc - 1)
    left(jwide, SEM_J + 1, nw - 1)
    left(jall, SEM_J + 2, nc - 1)


def per_device(sizes, conc_now, conc_prev, phi_prev, owner, partner, valence, diffusivity):
    nc, nw = sizes
    species, cx, nz, cy = conc_now.shape
    nb = nz // nc
    rows, modes = cx * nz, nc * cx * nb
    places, big, small = make_tables(nc, cx, nz, cy)
    ext = (cx + 2) * nz
    jrow = LEVELS * species // nc
    vmem = pl.BlockSpec(memory_space=pltpu.VMEM)
    hbm = pl.BlockSpec(memory_space=pltpu.HBM)
    sems = 3 * SWEEPS + 8 + 3
    fix = lambda x: pltpu.with_memory_space_constraint(x, pltpu.HBM)
    out_conc, out_phi = pl.pallas_call(
        functools.partial(kernel, (nc, nw, cx, nz, cy), places),
        out_shape=(
            jax.ShapeDtypeStruct((species * rows, cy), f32),
            jax.ShapeDtypeStruct((rows, cy), f32),
        ),
        in_specs=[hbm] * 9,
        out_specs=(vmem, vmem),
        scratch_shapes=[
            pltpu.SMEM((species,), jnp.int32),
            pltpu.SMEM((species,), f32),
            pltpu.VMEM((species * rows, cy), f32),
            pltpu.VMEM((species * rows, cy), f32),
            pltpu.VMEM((rows, cy), f32),
            pltpu.VMEM((rows, cy), jnp.int32),
            pltpu.VMEM((LEVELS, LANES), jnp.int32),
            pltpu.VMEM(big.shape, bf16),
            pltpu.VMEM(small.shape[1:], f32),
            pltpu.VMEM((ext, 2 * cy), f32),
            pltpu.VMEM((6, rows, cy), f32),
            pltpu.VMEM((2, 7, rows, cy), f32),
            pltpu.VMEM((species, 6, rows, cy), f32),
            pltpu.VMEM((rows, cy), f32),
            pltpu.VMEM((rows, cy), f32),
            pltpu.VMEM((2 * cy, 2 * modes), bf16),
            pltpu.VMEM((cy, 2 * modes), bf16),
            pltpu.VMEM((modes, 2 * modes), f32),
            pltpu.VMEM((modes, cy), f32),
            pltpu.VMEM((2 * modes, 2 * cy), bf16),
            pltpu.VMEM((2, nw, 2, modes), f32),
            pltpu.VMEM((SWEEPS, nc, cx * nb, cy), f32),
            pltpu.VMEM((SWEEPS, nc, cx * nb, cy), f32),
            pltpu.VMEM((SWEEPS, 2, modes), f32),
            pltpu.VMEM((SWEEPS, nw, 2, modes), f32),
            pltpu.VMEM((SWEEPS, nc, (cx + 2) * nb + 1, cy), f32),
            pltpu.VMEM((SWEEPS, nc, (cx + 2) * nb + 1, cy), f32),
            pltpu.VMEM((rows, cy), f32),
            pltpu.VMEM((2 * LEVELS, rows), f32),
            pltpu.VMEM((2, LEVELS, rows), f32),
            pltpu.VMEM((2, 2, nz, cy), f32),
            pltpu.VMEM((2, species, nz, cy), f32),
            pltpu.VMEM((LEVELS * (2 * species + 1), LANES), f32),
            pltpu.VMEM((nc, jrow, LANES), f32),
            pltpu.VMEM((nc, jrow, LANES), f32),
            pltpu.VMEM((jrow, LANES), f32),
            pltpu.VMEM((nw, jrow, LANES), f32),
            pltpu.VMEM((jrow, LANES), f32),
            pltpu.VMEM((nc, jrow, LANES), f32),
            pltpu.VMEM((2 * LEVELS * species, LANES), bf16),
            pltpu.VMEM((species * rows, cy), f32),
            pltpu.SemaphoreType.DMA((sems,)),
            pltpu.SemaphoreType.DMA((sems,)),
            pltpu.SemaphoreType.DMA((9,)),
            pltpu.SemaphoreType.REGULAR((2 + max(nw // 2 - 1, 1),)),
        ],
        compiler_params=pltpu.CompilerParams(
            collective_id=0, has_side_effects=True, vmem_limit_bytes=48 * 1024 * 1024
        ),
        name="step",
    )(
        *[fix(x) for x in (valence, diffusivity, conc_now.reshape(species * rows, cy), conc_prev.reshape(species * rows, cy), phi_prev.reshape(rows, cy), owner.reshape(rows, cy), partner.reshape(LEVELS, LANES), jnp.asarray(big), jnp.asarray(small))]
    )
    return out_conc.reshape(conc_now.shape), out_phi.reshape(phi_prev.shape)


def solution(mesh):
    return jax.shard_map(
        functools.partial(per_device, (mesh.shape["chan"], mesh.shape["wide"])),
        mesh=mesh,
        in_specs=(
            P(None, "chan", None, "wide"),
            P(None, "chan", None, "wide"),
            P("chan", None, "wide"),
            P("chan", None, "wide"),
            P(),
            P(),
            P(),
        ),
        out_specs=(P(None, "chan", None, "wide"), P("chan", None, "wide")),
        check_vma=False,
    )
```

```python
import functools

import jax
import jax.numpy as jnp
import numpy as np
from jax import lax
from jax.experimental import pallas as pl
from jax.experimental.pallas import tpu as pltpu
from jax.sharding import PartitionSpec as P

SWEEPS = 4
charge_scale = 0.05
coupling = 2.0
conduct_ref = 1.5
LANES = 128
LEVELS = 16
ROWS_AT_ONCE = 4
MESH = pl.DeviceIdType.MESH
f32 = jnp.float32
bf16 = jnp.bfloat16


def sine_table(length):
    index = np.arange(length) + 1.0
    return np.sqrt(2.0 / (length + 1.0)) * np.sin(np.pi * np.outer(index, index) / (length + 1.0))


def eigen_values(length):
    return 2.0 - 2.0 * np.cos(np.pi * (np.arange(length) + 1.0) / (length + 1.0))


def halves(table):
    table = np.asarray(table, np.float32)
    high = table.astype(bf16)
    low = (table - high.astype(np.float32)).astype(bf16)
    return high, low


def make_tables(nc, cx, nz, cy):
    nx, nb = nc * cx, nz // nc
    qx, qz, qy = sine_table(nx), sine_table(nz), sine_table(cy)
    depth_to = np.zeros((nc, cx, nb, cx, nz))
    for x in range(cx):
        depth_to[:, x, :, x, :] = qz.reshape(nc, nb, nz)
    length_to = np.einsum("aX,bc->abXc", qx, np.eye(nb)) / conduct_ref
    length_back = np.zeros((nc, cx + 2, nb, nx, nb))
    for p in range(nc):
        for xx in range(cx + 2):
            place = cx * p + xx - 1
            if 0 <= place < nx:
                for b in range(nb):
                    length_back[p, xx, b, :, b] = qx[place]
    depth_back = np.zeros((cx + 2, nz, nc, cx + 2, nb))
    for xx in range(cx + 2):
        depth_back[xx, :, :, xx, :] = qz.reshape(nz, nc, nb)
    depth_ring = np.zeros((cx, nz, cx, nb, nc))
    for x in range(cx):
        depth_ring[x, :, x, :, :] = qz.reshape(nz, nc, nb).transpose(0, 2, 1)
    length_ring = np.zeros((cx, nc, nx, nb))
    length_ring[:] = qx.reshape(nc, cx, nx).transpose(1, 0, 2)[..., None]
    lane_pick = np.zeros((cx, 2, nx, nb, cy))
    for x in range(cx):
        for b in range(nb):
            lane_pick[x, 0, :, b, (2 * (x * nb + b) - 1) % cy] = 1.0
            lane_pick[x, 1, :, b, 2 * (x * nb + b)] = 1.0
    modes = nx * nb
    lam = eigen_values(nx)[:, None] + eigen_values(nz)[None, :]
    lam = lam.reshape(nx, nc, nb).transpose(1, 0, 2).reshape(nc, 1, modes)
    theta = np.arccosh(1.0 + lam / 2.0)
    big = dict(
        dt=depth_to.reshape(nc * cx * nb, cx * nz),
        lt=length_to.reshape(modes, modes),
        lb=length_back.reshape(nc * (cx + 2) * nb, modes),
        db=depth_back.reshape((cx + 2) * nz, nc * (cx + 2) * nb),
        wy=qy,
        dr=depth_ring.reshape(cx * nz, cx * nb * nc),
        lr=length_ring.reshape(cx * nc, modes),
        lp=lane_pick.reshape(cx * 2 * modes, cy),
    )
    places, parts, row = {}, [], 0
    for name, table in big.items():
        pair = halves(table)
        if name in ("dt", "lt", "lb", "dr"):
            pair = (np.concatenate(pair, axis=1),)
        if name == "lr":
            pair = (np.concatenate(pair, axis=0),)
        if name == "lp":
            pair = pair[:1]
        for k, half in enumerate(pair):
            height = -(-half.shape[0] // 32) * 32
            block = np.zeros((height, 2 * LANES), bf16)
            block[: half.shape[0], : half.shape[1]] = half
            parts.append(block)
            places[name, k] = (row, *half.shape)
            row += height
    small = np.zeros((nc, 8, max(modes, LANES)), np.float32)
    small[:, 0, :modes] = theta[:, 0]
    small[:, 1, :modes] = lam[:, 0]
    small[:, 2, :cy] = eigen_values(cy)
    return places, np.concatenate(parts, axis=0), small


def dot(a, b):
    return jnp.dot(a, b, preferred_element_type=f32)


def split(value):
    high = value.astype(bf16)
    return high, (value - high.astype(f32)).astype(bf16)


def product(table, value):
    high, low = split(value)
    width = value.shape[1]
    found = dot(table[0], jnp.concatenate([high, low], axis=1))
    return found[:, :width] + found[:, width:] + dot(table[1], high)


def product_right(value, table):
    high, low = split(value)
    return dot(high, table[0]) + dot(high, table[1]) + dot(low, table[0])


def iota(shape, dim):
    return lax.broadcasted_iota(jnp.int32, shape, dim)


def kernel(
    cfg, places,
    val_hbm, dif_hbm, conc_hbm, prev_hbm, phi_hbm, own_hbm, par_hbm, big_hbm, small_hbm,
    out_conc, out_phi,
    val_ref, dif_ref, conc_ref, prev_ref, phi_ref, own_ref, par_ref, big, small,
    phi_e, faces, flows, beside, columns, charge, decay_h, decay_l, length_t, tab_d, edges, coef,
    send1, recv1, send_g, recv_g, send2, recv2,
    sig, cols, cols_in, plane_in, conc_in,
    jacc, jmean, jrecv, jsum, jwide, jpiece, jall, jtab, src,
    send_sem, recv_sem, load_sem, known,
):
    nc, nw, cx, nz, cy = cfg
    nb = nz // nc
    rows = cx * nz
    modes = nc * cx * nb
    species = conc_ref.shape[0] // rows
    me_c = lax.axis_index("chan")
    me_w = lax.axis_index("wide")
    left_c, right_c = lax.rem(me_c + nc - 1, nc), lax.rem(me_c + 1, nc)
    left_w, right_w = lax.rem(me_w + nw - 1, nw), lax.rem(me_w + 1, nw)

    barrier = pltpu.get_barrier_semaphore()

    if nc == 32:
        order = [(dx, dy, dc) for dx in range(4) for dy in range(4) for dc in range(2)]
        hops = (0, 1, 2, 1)
        order = sorted(order[1:], key=lambda o: -(hops[o[0]] + hops[o[1]]))
        at_x = [lax.rem(me_c // 8 + d, 4) * 8 for d in range(4)]
        at_y = [lax.rem(me_c // 2 + d, 4) * 2 for d in range(4)]
        at_core = [lax.rem(me_c + d, 2) for d in range(2)]
        peers_c = [at_x[dx] + at_y[dy] + at_core[dc] for dx, dy, dc in order]
    else:
        peers_c = [lax.rem(me_c + d, nc) for d in range(1, nc)]
    peers_w = [lax.rem(me_w + d, nw) for d in sorted(range(1, nw), key=lambda d: -min(d, nw - d))]

    dx_all, dy_all = {32: (4, 4), 8: (2, 2), 4: (2, 1)}[nc]
    core = lax.rem(me_c, 2)
    chip_y = lax.rem(me_c // 2, dy_all)
    chip_x = me_c // (2 * dy_all)
    chip = lambda x, y, c: (x * dy_all + y) * 2 + c
    partner_core = chip(chip_x, chip_y, 1 - core)
    beside_chip = jnp.where(core == 0, left_c, right_c)
    row_peers = [chip(lax.rem(chip_x + d, dx_all), chip_y, core) for d in range(1, dx_all)]
    column_peers = [chip(chip_x, lax.rem(chip_y + d, dy_all), core) for d in range(1, dy_all)]
    width_peers = [left_w, right_w] if nw > 2 else [right_w]

    def tell(semaphore, axis, peers):
        for p in peers:
            pl.semaphore_signal(semaphore, inc=1, device_id={axis: p}, device_id_type=MESH)

    tell(barrier, "wide", width_peers)
    tell(barrier, "chan", [beside_chip] + row_peers + column_peers + [partner_core])

    loads = {}
    for k, (name, there, here) in enumerate([
        ("conc", conc_hbm, conc_ref), ("val", val_hbm, val_ref), ("dif", dif_hbm, dif_ref),
        ("phi", phi_hbm, phi_ref), ("small", small_hbm.at[me_c], small), ("big", big_hbm, big),
        ("own", own_hbm, own_ref), ("par", par_hbm, par_ref), ("prev", prev_hbm, prev_ref),
    ]):
        loads[name] = pltpu.make_async_copy(there, here, load_sem.at[k])
        loads[name].start()

    def table(name):
        def half(k):
            row, height, width = places[name, k]
            return big[pl.ds(row, height), pl.ds(0, width)]
        return half(0), half(1)

    def twin(name):
        row, height, width = places[name, 0]
        return big[pl.ds(row, height), pl.ds(0, width)]

    def product_twin(name, value):
        both = twin(name)
        high, low = split(value)
        width = value.shape[1]
        value = jnp.concatenate(
            [jnp.concatenate([high, high], axis=0), jnp.concatenate([low, jnp.zeros_like(low)], axis=0)], axis=1
        )
        found = dot(both, value)
        return found[:, :width] + found[:, width:]

    lane = iota((rows, cy), 1)
    row = iota((rows, cy), 0)
    depth = lax.rem(row, nz)
    at_first, at_last = lane == 0, lane == cy - 1
    top, bottom = depth == 0, depth == nz - 1

    for name in ("val", "dif", "conc"):
        loads[name].wait()
    val = [val_ref[s].astype(f32) for s in range(species)]
    dif = [dif_ref[s] for s in range(species)]
    total = jnp.zeros((rows, cy), f32)
    part = jnp.zeros((rows, cy), f32)
    weight_all = jnp.float32(0.0)
    for s in range(species):
        c = conc_ref[pl.ds(s * rows, rows), :]
        square = val[s] * val[s]
        weight_all = weight_all + (square + 1.0) * dif[s]
        part = part + (square * dif[s]) * c * c
        total = total + val[s] * c
    sigma = 1.0 + part / jnp.full((1, 1), weight_all, f32)
    sig[...] = sigma
    loads["phi"].wait()
    phi = phi_ref[...]

    packed = jnp.zeros((rows, cy), f32)
    for k in range(species + 2):
        field = phi if k == 0 else sigma if k == 1 else conc_ref[pl.ds((k - 2) * rows, rows), :]
        packed = jnp.where(lane == k, pltpu.roll(field, k, 1) if k else field, packed)
        packed = jnp.where(lane == LEVELS + k, pltpu.roll(field, LEVELS + 1 + k, 1), packed)
    cols[...] = packed.T[: 2 * LEVELS]

    pl.semaphore_wait(barrier, 2 + len(row_peers) + len(column_peers) + len(width_peers))

    SEM_A, SEM_G, SEM_B = 0, SWEEPS, 2 * SWEEPS
    SEM_H = 3 * SWEEPS
    SEM_J = SEM_H + 8

    def remote(src, dst, k, axis, place):
        return pltpu.make_async_remote_copy(
            src_ref=src, dst_ref=dst, send_sem=send_sem.at[k], recv_sem=recv_sem.at[k],
            device_id={axis: place}, device_id_type=MESH,
        )

    halo = [
        remote(cols.at[pl.ds(0, LEVELS)], cols_in.at[1], SEM_H, "wide", left_w),
        remote(cols.at[pl.ds(LEVELS, LEVELS)], cols_in.at[0], SEM_H + 1, "wide", right_w),
        remote(sig.at[pl.ds(0, nz)], plane_in.at[1, 0], SEM_H + 2, "chan", left_c),
        remote(sig.at[pl.ds(rows - nz, nz)], plane_in.at[0, 0], SEM_H + 3, "chan", right_c),
        remote(phi_ref.at[pl.ds(0, nz)], plane_in.at[1, 1], SEM_H + 4, "chan", left_c),
        remote(phi_ref.at[pl.ds(rows - nz, nz)], plane_in.at[0, 1], SEM_H + 5, "chan", right_c),
    ]
    conc_halo = []
    for s in range(species):
        conc_halo += [
            remote(conc_ref.at[pl.ds(s * rows, nz)], conc_in.at[1, s], SEM_H + 6, "chan", left_c),
            remote(conc_ref.at[pl.ds((s + 1) * rows - nz, nz)], conc_in.at[0, s], SEM_H + 7, "chan", right_c),
        ]
    for copy in halo:
        copy.start()

    far_steps = nw // 2 - 1

    def known_w(k):
        if k > 0 and k <= far_steps:
            pl.semaphore_wait(known.at[1 + k], len(width_peers))
        if k < far_steps:
            tell(known.at[2 + k], "wide", width_peers)

    tell(known.at[0], "chan", row_peers)
    known_w(0)

    def spread(src, dst, k, axis):
        n, me = (nc, me_c) if axis == "chan" else (nw, me_w)

        def body(i, _):
            p = lax.rem(me + i, n)
            remote(src(p), dst.at[me], k, axis, p).start()
            return 0

        lax.fori_loop(1, n, body, 0)
        pltpu.make_async_copy(src(me), dst.at[me], recv_sem.at[k]).start()

    def spread_fast(src, dst, k, axis):
        peers, me = (peers_c, me_c) if axis == "chan" else (peers_w, me_w)
        for p in peers:
            remote(src(p), dst.at[me], k, axis, p).start()
        pltpu.make_async_copy(src(me), dst.at[me], recv_sem.at[k]).start()

    def arrived(dst, k):
        pltpu.make_async_copy(dst, dst, recv_sem.at[k]).wait()

    def left(ref, k, n):
        part_of = ref.at[pl.ds(0, n)]
        pltpu.make_async_copy(part_of, part_of, send_sem.at[k]).wait()

    charge[...] = charge_scale * total
    loads["small"].wait()
    theta_row = small[0:1, 0:modes]
    theta = jnp.broadcast_to(theta_row, (cy, modes)).T
    lam = jnp.broadcast_to(small[1:2, 0:modes], (cy, modes)).T
    tab_d[...] = 1.0 / (lam + small[2:3, 0:cy])
    place = iota((modes, cy), 1).astype(f32)
    power = lambda n: jnp.exp(-theta * n)
    down = iota((cy, modes), 0).astype(f32)
    high, low = split(jnp.concatenate([jnp.exp(-theta_row * down), jnp.exp(-theta_row * (cy - 1.0 - down))], axis=1))
    decay_h[...] = jnp.concatenate([high, high], axis=0)
    decay_l[...] = low
    scale = 1.0 / (1.0 - power(2.0 * cy + 2.0))
    edge_left = (power(place + 1.0) - power(2.0 * cy + 1.0 - place)) * scale
    edge_right = (power(cy - place) - power(cy + 2.0 + place)) * scale
    for k, edge in enumerate((edge_left, edge_right)):
        high, low = split(edge)
        here = pl.ds(k * modes, modes)
        edges[here, 0:cy] = high
        edges[here, cy : 2 * cy] = low
    width1 = cy * nw + 1
    rowp = lambda n: jnp.exp(-theta_row * n)
    front = 1.0 / ((1.0 - rowp(2.0)) * (1.0 - rowp(2.0 * width1)))
    for k in range(2):
        at = (cy * me_w if k == 0 else cy * (me_w + 1) + 1).astype(f32)
        below = (1.0 - rowp(2.0 * (width1 - at))) * front
        above = (1.0 - rowp(2.0 * at)) * front
        for w in range(nw):
            lower = (w < me_w) if k == 0 else (w <= me_w)
            n_plus = jnp.where(lower, at + (cy * w + 2.0), cy * w + 2.0 - at)
            n_minus = jnp.where(lower, at - (cy * w + cy - 1.0), 2.0 * width1 - at - (cy * w + cy - 1.0))
            factor = jnp.where(lower, below, above)
            sign = jnp.where(lower, -1.0, 1.0)
            coef[k, w, 0:1, :] = sign * factor * rowp(n_plus)
            coef[k, w, 1:2, :] = -sign * factor * rowp(n_minus)

    pl.semaphore_wait(known.at[0], len(row_peers))
    tell(known.at[1], "chan", [partner_core])
    known_w(1)
    jacc[...] = jnp.zeros_like(jacc)
    faces[2] = 0.5 * (sigma + jnp.where(top, 0.0, pltpu.roll(sigma, 1, 0)))
    faces[3] = 0.5 * (sigma + jnp.where(bottom, 0.0, pltpu.roll(sigma, rows - 1, 0)))

    loads["big"].wait()
    length = twin("lt")
    length = (length[:, :modes].astype(f32) + length[:, modes:].astype(f32)).T
    length_t[...] = jnp.concatenate([length, length], axis=1)

    for copy in halo[:2]:
        copy.wait_recv()
    known_w(2)
    wall_xl, wall_xr = me_c == 0, me_c == nc - 1
    wall_yl, wall_yr = me_w == 0, me_w == nw - 1
    keep_xl, keep_xr = jnp.where(wall_xl, 0.0, 1.0), jnp.where(wall_xr, 0.0, 1.0)
    keep_yl, keep_yr = jnp.where(wall_yl, 0.0, 1.0), jnp.where(wall_yr, 0.0, 1.0)
    stacked = jnp.concatenate(
        [cols_in[0], cols_in[1], jnp.zeros((cy - 2 * LEVELS, rows), f32)], axis=0
    )
    col_in = stacked.T
    columns[...] = col_in

    def neighbours(field, plane_l, plane_r, col_l, col_r, edge):
        low = field if edge is None else jnp.zeros_like(field)
        return [
            jnp.concatenate([plane_l, field[: rows - nz]], axis=0),
            jnp.concatenate([field[nz:], plane_r], axis=0),
            jnp.where(top, low, pltpu.roll(field, 1, 0)),
            jnp.where(bottom, low, pltpu.roll(field, rows - 1, 0)),
            jnp.where(at_first, col_l, pltpu.roll(field, 1, 1)),
            jnp.where(at_last, col_r, pltpu.roll(field, cy - 1, 1)),
        ]

    edge_l, edge_r = col_in[:, 1:2] * keep_yl, col_in[:, LEVELS + 1 : LEVELS + 2] * keep_yr
    faces[4] = 0.5 * (sigma + jnp.where(at_first, edge_l, pltpu.roll(sigma, 1, 1)))
    faces[5] = 0.5 * (sigma + jnp.where(at_last, edge_r, pltpu.roll(sigma, cy - 1, 1)))
    phi_e[nz : nz + rows, 0:cy] = phi
    phi_e[0:nz, cy : 2 * cy] = jnp.zeros((nz, cy), f32)
    phi_e[nz + rows : 2 * nz + rows, cy : 2 * cy] = jnp.zeros((nz, cy), f32)
    zero = jnp.zeros((rows, cy), f32)
    phi_e[nz : nz + rows, cy : 2 * cy] = jnp.where(
        at_last, col_in[:, 0:1] * keep_yl, jnp.where(at_first, col_in[:, LEVELS : LEVELS + 1] * keep_yr, zero)
    )
    for copy in halo[2:]:
        copy.wait_recv()
    faces[0] = 0.5 * (sigma + jnp.concatenate([plane_in[0, 0] * keep_xl, sigma[: rows - nz]], axis=0))
    faces[1] = 0.5 * (sigma + jnp.concatenate([sigma[nz:], plane_in[1, 0] * keep_xr], axis=0))
    phi_e[0:nz, 0:cy] = plane_in[0, 1] * keep_xl
    phi_e[nz + rows : 2 * nz + rows, 0:cy] = plane_in[1, 1] * keep_xr

    def phi_near(beyond):
        field = phi_e[nz : nz + rows, 0:cy]
        ring = phi_e[nz : nz + rows, cy : 2 * cy]
        low = field if beyond is None else jnp.zeros_like(field)
        return field, [
            phi_e[0:rows, 0:cy],
            phi_e[2 * nz : 2 * nz + rows, 0:cy],
            jnp.where(top, low, pltpu.roll(field, 1, 0)),
            jnp.where(bottom, low, pltpu.roll(field, rows - 1, 0)),
            pltpu.roll(jnp.where(at_last, ring, field), 1, 1),
            pltpu.roll(jnp.where(at_first, ring, field), cy - 1, 1),
        ]

    def one_hot(label):
        return jnp.where(iota((LANES, LANES), 0) == (label & (LANES - 1)), 1.0, 0.0).astype(bf16)

    def sum_rows(first, last):
        def body(i, acc):
            picks, values = [], []
            for t in range(ROWS_AT_ONCE):
                r = i * ROWS_AT_ONCE + t
                label = own_ref[pl.ds(r, 1), :]
                level = lax.shift_right_logical(label, 7)
                value = conc_ref[pl.ds(r, species, stride=rows), :]
                high = value.astype(bf16).astype(f32)
                low = value - high
                picks.append(one_hot(label))
                here = [level == n for n in range(LEVELS)]
                blocks = [jnp.where(here[n], high, 0.0) for n in range(LEVELS)]
                blocks += [jnp.where(here[n], low, 0.0) for n in range(LEVELS)]
                blocks.append(jnp.where(iota((LEVELS, LANES), 0) == level, 1.0, 0.0))
                values.append(jnp.concatenate(blocks, axis=0).astype(bf16))
            jacc[...] += lax.dot_general(
                jnp.concatenate(values, axis=1), jnp.concatenate(picks, axis=1),
                (((1,), (1,)), ((), ())), preferred_element_type=f32,
            )
            return acc

        lax.fori_loop(first // ROWS_AT_ONCE, last // ROWS_AT_ONCE, body, 0)

    def look_up(table, labels):
        pick = jnp.concatenate([one_hot(label) for label in labels], axis=1)
        found = dot(table, pick)
        half = LEVELS * species
        results = []
        for t, label in enumerate(labels):
            level = lax.shift_right_logical(label, 7)
            column = found[:, t * LANES : (t + 1) * LANES]
            result = jnp.zeros((species, LANES), f32)
            for n in range(LEVELS):
                both = column[n * species : (n + 1) * species] + column[half + n * species : half + (n + 1) * species]
                result = result + jnp.where(level == n, both, 0.0)
            results.append(result)
        return results

    def means():
        half = LEVELS * species
        count = jnp.maximum(jacc[2 * half : 2 * half + LEVELS, :], 1.0)
        blocks = []
        for n in range(LEVELS):
            here = slice(n * species, (n + 1) * species)
            there = slice(half + n * species, half + (n + 1) * species)
            blocks.append((jacc[here, :] + jacc[there, :]) / count[n : n + 1])
        jmean[...] = jnp.concatenate(blocks, axis=0).reshape(jmean.shape)
        spread(lambda p: jmean.at[p], jrecv, SEM_J, "chan")

    def means_chan():
        arrived(jrecv, SEM_J)
        jsum[...] = jnp.sum(jrecv[...], axis=0)
        spread(lambda p: jsum, jwide, SEM_J + 1, "wide")

    def means_wide():
        arrived(jwide, SEM_J + 1)
        jpiece[...] = jnp.sum(jwide[...], axis=0)
        spread(lambda p: jpiece, jall, SEM_J + 2, "chan")

    def junction_table():
        arrived(jall, SEM_J + 2)
        table = jall[...].reshape(LEVELS * species, LANES)
        both = jnp.concatenate(split(table), axis=0)
        blocks = []
        for n in range(0, LEVELS, 2):
            found = look_up(both, [par_ref[n : n + 1, :], par_ref[n + 1 : n + 2, :]])
            for t in range(2):
                here = slice((n + t) * species, (n + t + 1) * species)
                blocks.append(coupling * (found[t] - table[here]))
        jtab[...] = jnp.concatenate(split(jnp.concatenate(blocks, axis=0)), axis=0)

    def source_rows(first, last):
        def body(i, acc):
            labels = [own_ref[pl.ds(i * ROWS_AT_ONCE + t, 1), :] for t in range(ROWS_AT_ONCE)]
            for t, found in enumerate(look_up(jtab[...], labels)):
                src[pl.ds(i * ROWS_AT_ONCE + t, species, stride=rows), :] = found
            return acc

        lax.fori_loop(first // ROWS_AT_ONCE, last // ROWS_AT_ONCE, body, 0)

    def conc_near(s):
        c = conc_ref[pl.ds(s * rows, rows), :]
        plane_l = jnp.where(wall_xl, c[:nz], conc_in[0, s])
        plane_r = jnp.where(wall_xr, c[rows - nz :], conc_in[1, s])
        col_l = jnp.where(wall_yl, c, columns[:, s + 2 : s + 3])
        col_r = jnp.where(wall_yr, c, columns[:, LEVELS + s + 2 : LEVELS + s + 3])
        return c, neighbours(c, plane_l, plane_r, col_l, col_r, None)

    def start_species():
        loads["prev"].wait()
        arrived(conc_in.at[1], SEM_H + 6)
        arrived(conc_in.at[0], SEM_H + 7)
        for s in range(species):
            c, near_c = conc_near(s)
            flow = near_c[0]
            for k in range(6):
                beside[s, k] = near_c[k]
                flow = flow + near_c[k] if k else flow
            here = pl.ds(s * rows, rows)
            src[here, :] = src[here, :] + (4.0 * c - prev_ref[here, :]) + dif[s] * flow

    quarter = rows // 4

    def fill(sweep, spot):
        if sweep == 0:
            if spot == 1:
                for copy in conc_halo:
                    copy.start()
            if spot == 0:
                loads["own"].wait()
            sum_rows((0, quarter, 2 * quarter)[spot], (quarter, 2 * quarter, 3 * quarter)[spot])
        elif sweep == 1:
            if spot == 0:
                sum_rows(3 * quarter, rows)
                means()
            elif spot == 1:
                means_chan()
            else:
                means_wide()
        elif sweep == 2:
            if spot == 0:
                loads["par"].wait()
                junction_table()
            elif spot == 1:
                source_rows(0, quarter)
            else:
                source_rows(quarter, 2 * quarter)
        else:
            if spot == 0:
                source_rows(2 * quarter, 3 * quarter)
            elif spot == 1:
                source_rows(3 * quarter, rows)
            else:
                start_species()


    pl.semaphore_wait(known.at[1], 1)

    for sweep in range(SWEEPS):
        field, near = phi_near(0)
        residual = charge[...]
        for k in range(6):
            residual = residual - faces[k] * (field - near[k])
        send1[sweep] = product_twin("dt", residual).reshape(send1.shape[1:])
        spread_fast(lambda p: send1.at[sweep, p], recv1.at[sweep], SEM_A + sweep, "chan")
        fill(sweep, 0)
        arrived(recv1.at[sweep], SEM_A + sweep)
        arrival = recv1[sweep].reshape(modes, cy)
        high, low = split(arrival)
        decayed = dot(jnp.concatenate([high, low], axis=1), decay_h[...]) + dot(high, decay_l[...])
        moments = jnp.sum(decayed * length_t[...], axis=0, keepdims=True)
        send_g[sweep, 0:1, :] = moments[:, :modes]
        send_g[sweep, 1:2, :] = moments[:, modes:]
        if sweep == 0:
            for k in range(3, far_steps + 1):
                known_w(k)
        spread_fast(lambda p: send_g.at[sweep], recv_g.at[sweep], SEM_G + sweep, "wide")
        force = product_twin("lt", arrival)
        width = table("wy")
        inner = product_right(product_right(force, width) * tab_d[...], width)
        inner = product_twin("lb", inner)
        fill(sweep, 1)
        arrived(recv_g.at[sweep], SEM_G + sweep)
        got = recv_g[sweep]
        ends = [jnp.sum(jnp.sum(got * coef[k], axis=0), axis=0, keepdims=True) for k in range(2)]
        back = twin("lb")
        back = back[:, :modes].astype(f32) + back[:, modes:].astype(f32)
        high, low = split(jnp.concatenate([back * ends[0], back * ends[1]], axis=1))
        outer = dot(high, edges[...])
        outer = inner + outer[:, :cy] + outer[:, cy:] + dot(low, edges[:, 0:cy])
        span = (cx + 2) * nb
        send2[sweep, :, 0:span, :] = outer.reshape(nc, span, cy)
        lines = twin("lr")
        lines = lines[: nc * cx].astype(f32) + lines[nc * cx :].astype(f32)
        lines = jnp.concatenate([lines[x * nc : (x + 1) * nc] * end for x in range(cx) for end in ends], axis=1)
        high, low = split(lines)
        ring = dot(high, twin("lp")) + dot(low, twin("lp"))
        send2[sweep, :, span : span + 1, :] = ring.reshape(nc, 1, cy)
        spread_fast(lambda p: send2.at[sweep, p], recv2.at[sweep], SEM_B + sweep, "chan")
        fill(sweep, 2)
        arrived(recv2.at[sweep], SEM_B + sweep)
        phi_e[:, 0:cy] += product(table("db"), recv2[sweep, :, 0:span, :].reshape(nc * span, cy))
        ring = recv2[sweep, :, span : span + 1, :].reshape(nc, cy)
        pieces = [pltpu.roll(ring, cy - 2 * j, 1) if j else ring for j in range(cx * nb)]
        phi_e[nz : nz + rows, cy : 2 * cy] += product_twin("dr", jnp.concatenate(pieces, axis=0))

    field, near = phi_near(None)
    out_phi[...] = field
    drops = []
    for k in range(6):
        drop = field - near[k]
        if k == 0:
            drop = jnp.where((row < nz) & wall_xl, 0.0, drop)
        elif k == 1:
            drop = jnp.where((row >= rows - nz) & wall_xr, 0.0, drop)
        elif k == 4:
            drop = jnp.where(at_first & wall_yl, 0.0, drop)
        elif k == 5:
            drop = jnp.where(at_last & wall_yr, 0.0, drop)
        drops.append(drop)
    outs = [jnp.zeros((rows, cy), f32)] * 2
    for k in range(6):
        up, down = jnp.maximum(drops[k], 0.0), jnp.maximum(-drops[k], 0.0)
        flows[0, k], flows[1, k] = down, up
        outs = [outs[0] + up, outs[1] + down]
    flows[0, 6], flows[1, 6] = outs
    for s in range(species):
        sign = jnp.where(val_ref[s] < 0, 1, 0)
        drift = jnp.abs(val[s] * dif[s])
        inward = flows[sign, 0] * beside[s, 0]
        for k in range(1, 6):
            inward = inward + flows[sign, k] * beside[s, k]
        here = pl.ds(s * rows, rows)
        out_conc[here, :] = (src[here, :] + drift * inward) / ((3.0 + 6.0 * dif[s]) + drift * flows[sign, 6])

    for copy in halo:
        copy.wait_send()
    for k in (6, 7):
        pltpu.make_async_copy(conc_in.at[0], conc_in.at[0], send_sem.at[SEM_H + k]).wait()
    for sweep in range(SWEEPS):
        left(send1.at[sweep], SEM_A + sweep, nc - 1)
        left(recv_g.at[sweep], SEM_G + sweep, nw - 1)
        left(send2.at[sweep], SEM_B + sweep, nc - 1)
    left(jmean, SEM_J, nc - 1)
    left(jwide, SEM_J + 1, nw - 1)
    left(jall, SEM_J + 2, nc - 1)


def per_device(sizes, conc_now, conc_prev, phi_prev, owner, partner, valence, diffusivity):
    nc, nw = sizes
    species, cx, nz, cy = conc_now.shape
    nb = nz // nc
    rows, modes = cx * nz, nc * cx * nb
    places, big, small = make_tables(nc, cx, nz, cy)
    ext = (cx + 2) * nz
    jrow = LEVELS * species // nc
    vmem = pl.BlockSpec(memory_space=pltpu.VMEM)
    hbm = pl.BlockSpec(memory_space=pltpu.HBM)
    sems = 3 * SWEEPS + 8 + 3
    fix = lambda x: pltpu.with_memory_space_constraint(x, pltpu.HBM)
    out_conc, out_phi = pl.pallas_call(
        functools.partial(kernel, (nc, nw, cx, nz, cy), places),
        out_shape=(
            jax.ShapeDtypeStruct((species * rows, cy), f32),
            jax.ShapeDtypeStruct((rows, cy), f32),
        ),
        in_specs=[hbm] * 9,
        out_specs=(vmem, vmem),
        scratch_shapes=[
            pltpu.SMEM((species,), jnp.int32),
            pltpu.SMEM((species,), f32),
            pltpu.VMEM((species * rows, cy), f32),
            pltpu.VMEM((species * rows, cy), f32),
            pltpu.VMEM((rows, cy), f32),
            pltpu.VMEM((rows, cy), jnp.int32),
            pltpu.VMEM((LEVELS, LANES), jnp.int32),
            pltpu.VMEM(big.shape, bf16),
            pltpu.VMEM(small.shape[1:], f32),
            pltpu.VMEM((ext, 2 * cy), f32),
            pltpu.VMEM((6, rows, cy), f32),
            pltpu.VMEM((2, 7, rows, cy), f32),
            pltpu.VMEM((species, 6, rows, cy), f32),
            pltpu.VMEM((rows, cy), f32),
            pltpu.VMEM((rows, cy), f32),
            pltpu.VMEM((2 * cy, 2 * modes), bf16),
            pltpu.VMEM((cy, 2 * modes), bf16),
            pltpu.VMEM((modes, 2 * modes), f32),
            pltpu.VMEM((modes, cy), f32),
            pltpu.VMEM((2 * modes, 2 * cy), bf16),
            pltpu.VMEM((2, nw, 2, modes), f32),
            pltpu.VMEM((SWEEPS, nc, cx * nb, cy), f32),
            pltpu.VMEM((SWEEPS, nc, cx * nb, cy), f32),
            pltpu.VMEM((SWEEPS, 2, modes), f32),
            pltpu.VMEM((SWEEPS, nw, 2, modes), f32),
            pltpu.VMEM((SWEEPS, nc, (cx + 2) * nb + 1, cy), f32),
            pltpu.VMEM((SWEEPS, nc, (cx + 2) * nb + 1, cy), f32),
            pltpu.VMEM((rows, cy), f32),
            pltpu.VMEM((2 * LEVELS, rows), f32),
            pltpu.VMEM((2, LEVELS, rows), f32),
            pltpu.VMEM((2, 2, nz, cy), f32),
            pltpu.VMEM((2, species, nz, cy), f32),
            pltpu.VMEM((LEVELS * (2 * species + 1), LANES), f32),
            pltpu.VMEM((nc, jrow, LANES), f32),
            pltpu.VMEM((nc, jrow, LANES), f32),
            pltpu.VMEM((jrow, LANES), f32),
            pltpu.VMEM((nw, jrow, LANES), f32),
            pltpu.VMEM((jrow, LANES), f32),
            pltpu.VMEM((nc, jrow, LANES), f32),
            pltpu.VMEM((2 * LEVELS * species, LANES), bf16),
            pltpu.VMEM((species * rows, cy), f32),
            pltpu.SemaphoreType.DMA((sems,)),
            pltpu.SemaphoreType.DMA((sems,)),
            pltpu.SemaphoreType.DMA((9,)),
            pltpu.SemaphoreType.REGULAR((2 + max(nw // 2 - 1, 1),)),
        ],
        compiler_params=pltpu.CompilerParams(
            collective_id=0, has_side_effects=True, vmem_limit_bytes=48 * 1024 * 1024
        ),
        name="step",
    )(
        *[fix(x) for x in (valence, diffusivity, conc_now.reshape(species * rows, cy), conc_prev.reshape(species * rows, cy), phi_prev.reshape(rows, cy), owner.reshape(rows, cy), partner.reshape(LEVELS, LANES), jnp.asarray(big), jnp.asarray(small))]
    )
    return out_conc.reshape(conc_now.shape), out_phi.reshape(phi_prev.shape)


def solution(mesh):
    return jax.shard_map(
        functools.partial(per_device, (mesh.shape["chan"], mesh.shape["wide"])),
        mesh=mesh,
        in_specs=(
            P(None, "chan", None, "wide"),
            P(None, "chan", None, "wide"),
            P("chan", None, "wide"),
            P("chan", None, "wide"),
            P(),
            P(),
            P(),
        ),
        out_specs=(P(None, "chan", None, "wide"), P("chan", None, "wide")),
        check_vma=False,
    )
```
